256 devices in a mesh: row: 16 (over y, x), col: 16 (over z, core).
Axes of the slice: x: 4, y: 4, z: 8, core: 2. Of those that a mesh axis runs over, the one named last changes fastest.
Arguments:
- block_values: float32 [16, 16, 40, 128, 128], P('row', 'col'), may hold values from 7.8125e-06 to 0.00078125
- block_index: int32 [16, 16, 2, 40], P('row', 'col'), may hold values from 0 to 31, as said below
- block_count: int32 [16, 16], P('row', 'col'), may hold values from 1 to 40, as said below
- strength: float32 [32], replicated, may hold values from 1 to 30
- raw_scores: float32 [512, 32, 128], P(('row', 'col')), may hold values from -24 to 24
Outputs:
- smoothed: float32 [512, 32, 128], P(('row', 'col'))
- final_residual: float32 [512, 32, 128], P(('row', 'col'))
The draws below stay inside these ranges and needn't reach their ends.
Inputs may be any that keep to these rules, and one draw needn't show every extreme that they name: `block_count`: some device has exactly 40 live slots; the others hold between half and all of their share of the upper triangle, scaled to 40. `block_index`: the live slots of one device name distinct blocks, each with global block row at most its global block column; slots at or above the count hold pairs in range that are ignored.
All inputs are finite; a program needn't handle non-finite values.
Results may differ from the reference program's by a relative error of at most 0.0003.
Values sent between devices are 32-bit elements; how exact they have to be, the bound alone decides.
A program may use at most 64 MiB of HBM per device.

```python
import math
import jax
import jax.numpy as jnp
from jax import lax

BS = 128
RHS = 32
SEG = 2
ITERS = 3
CAP = 40
NB = 512
N_ROW = 16
N_COL = 16


def block_pattern(key):
    rows_here = N_COL * SEG
    cols_here = N_ROW * SEG
    row_ids = jnp.arange(N_ROW, dtype=jnp.int32)[:, None, None, None]
    col_ids = jnp.arange(N_COL, dtype=jnp.int32)[None, :, None, None]
    local_rows = jnp.arange(rows_here, dtype=jnp.int32)[None, None, :, None]
    local_cols = jnp.arange(cols_here, dtype=jnp.int32)[None, None, None, :]
    global_rows = row_ids * rows_here + local_rows
    global_cols = (local_cols // SEG * N_COL + col_ids) * SEG + local_cols % SEG
    valid = (global_rows <= global_cols).astype(jnp.int32)
    valid_count = jnp.sum(valid, axis=(2, 3))
    top_count = jnp.max(valid_count)
    share_count = jnp.maximum(1, CAP * valid_count // top_count)
    cut = jax.random.randint(jax.random.fold_in(key, 13), (N_ROW, N_COL), 0, share_count // 2 + 1, dtype=jnp.int32)
    live_count = jnp.clip(share_count - cut, 1, CAP)
    flat_pos = jnp.arange(N_ROW * N_COL, dtype=jnp.int32).reshape(N_ROW, N_COL)
    busiest = jnp.argmax(valid_count.reshape(-1)).astype(jnp.int32)
    live_count = jnp.where(flat_pos == busiest, CAP, live_count)
    cells = rows_here * cols_here
    flat_valid = valid.reshape(N_ROW, N_COL, cells)
    split_keys = jax.random.split(jax.random.fold_in(key, 11), N_ROW * N_COL)
    shuffled = jax.vmap(lambda one_key: jax.random.permutation(one_key, cells))(split_keys).reshape(N_ROW, N_COL, cells).astype(jnp.int32)
    flat_index = jnp.arange(cells, dtype=jnp.int32)[None, None, :]
    scores = jnp.where(flat_valid > 0, shuffled + 1, -(flat_index + 1))
    _, chosen = lax.top_k(scores, CAP)
    chosen = chosen.astype(jnp.int32)
    index_pairs = jnp.stack([chosen // cols_here, chosen % cols_here], axis=2)
    return (index_pairs, live_count.astype(jnp.int32))


def draw_block_index(key, part):
    index_pairs, live_count = block_pattern(jax.random.fold_in(key, 5))
    return index_pairs


def draw_block_count(key, part):
    index_pairs, live_count = block_pattern(jax.random.fold_in(key, 5))
    return live_count


def draw_raw_scores(key, part):
    ramp = (3.0 ** (jnp.arange(NB, dtype=jnp.float32) / NB))[:, None, None]
    base = jnp.clip(jax.random.normal(jax.random.fold_in(key, 23), (NB, RHS, BS), jnp.float32), -6.0, 6.0)
    return base * ramp


def block_levels(own_key, dims, cuts, smallest, largest):
    def one(dim, parts):
        steps = jax.random.uniform(jax.random.fold_in(jax.random.fold_in(own_key, 6), dim), (parts,), jnp.float32, smallest / len(cuts), largest / len(cuts))
        return jnp.repeat(jnp.exp(steps), dims[dim] // parts).reshape((-1,) + (1,) * (len(dims) - dim - 1))

    factor_of = one(*cuts[0])
    for cut in cuts[1:]:
        factor_of = factor_of * one(*cut)
    return factor_of


def setup_inputs(seed: int = 0) -> dict:
    splits = jax.random.split(jax.random.key(seed), 6)
    return {
        "block_values": jnp.clip(jnp.exp(math.log(0.00078125) - 4.6051702 * jax.random.uniform(splits[0], (N_ROW, N_COL, CAP, BS, BS), jnp.float32) ** block_levels(splits[0], (N_ROW, N_COL, CAP, BS, BS), ((0, 16), (1, 16)), -0.2, 0.2)), 7.812500371073838e-06, 0.00078125),
        "block_index": draw_block_index(jax.random.fold_in(splits[5], 71), 0),
        "block_count": draw_block_count(jax.random.fold_in(splits[5], 71), 0),
        "strength": jnp.clip(jnp.exp(jax.random.uniform(splits[3], (RHS,), jnp.float32, math.log(1.0), math.log(30.0))), 1.0, 30.0),
        "raw_scores": draw_raw_scores(jax.random.fold_in(splits[5], 71), 0),
    }


def local_terms(values, row_index, col_index, panel_rows, panel_cols):
    picked_cols = jnp.take(panel_cols, col_index, axis=0)
    picked_rows = jnp.take(panel_rows, row_index, axis=0)
    to_rows = jnp.einsum("crk,cik->cri", picked_cols, values, precision=lax.Precision.HIGHEST)
    to_cols = jnp.einsum("cri,cik->crk", picked_rows, values, precision=lax.Precision.HIGHEST)
    row_part = jax.ops.segment_sum(to_rows, row_index, num_segments=panel_rows.shape[0])
    col_part = jax.ops.segment_sum(to_cols, col_index, num_segments=panel_cols.shape[0])
    return row_part, col_part


def apply_graph(vector, block_values, block_index, block_count):
    width = vector.shape[1]
    panel_grid = vector.reshape(N_ROW, N_COL, SEG, width, BS)

    def device_step(total_sum, device):
        row_pos = device // N_COL
        col_pos = device % N_COL
        panel_rows = lax.dynamic_index_in_dim(panel_grid, row_pos, 0, keepdims=False).reshape(N_COL * SEG, width, BS)
        panel_cols = lax.dynamic_index_in_dim(panel_grid, col_pos, 1, keepdims=False).reshape(N_ROW * SEG, width, BS)
        device_values = lax.dynamic_index_in_dim(lax.dynamic_index_in_dim(block_values, row_pos, 0, keepdims=False), col_pos, 0, keepdims=False)
        device_index = lax.dynamic_index_in_dim(lax.dynamic_index_in_dim(block_index, row_pos, 0, keepdims=False), col_pos, 0, keepdims=False)
        device_count = lax.dynamic_index_in_dim(lax.dynamic_index_in_dim(block_count, row_pos, 0, keepdims=False), col_pos, 0, keepdims=False)
        live_mask = (jnp.arange(CAP, dtype=jnp.int32) < device_count.astype(jnp.int32)).astype(jnp.float32)
        masked = device_values * live_mask[:, None, None]
        row_part, col_part = local_terms(masked, device_index[0].astype(jnp.int32), device_index[1].astype(jnp.int32), panel_rows, panel_cols)
        row_slab = lax.dynamic_index_in_dim(total_sum, row_pos, 0, keepdims=False) + row_part.reshape(N_COL, SEG, width, BS)
        total_sum = lax.dynamic_update_index_in_dim(total_sum, row_slab, row_pos, 0)
        col_slab = lax.dynamic_index_in_dim(total_sum, col_pos, 1, keepdims=False) + col_part.reshape(N_ROW, SEG, width, BS)
        total_sum = lax.dynamic_update_index_in_dim(total_sum, col_slab, col_pos, 1)
        return total_sum, None

    start = jnp.zeros((N_ROW, N_COL, SEG, width, BS), jnp.float32)
    total_sum, _ = lax.scan(device_step, start, jnp.arange(N_ROW * N_COL, dtype=jnp.int32))
    return total_sum.reshape(NB, width, BS)


def reference(block_values, block_index, block_count, strength, raw_scores):
    degree = apply_graph(jnp.ones((NB, 1, BS), jnp.float32), block_values, block_index, block_count)

    def operator(field):
        return field + strength[None, :, None] * (degree * field - apply_graph(field, block_values, block_index, block_count))

    def total(field):
        return jnp.sum(field, axis=(0, 2))

    smoothed = jnp.zeros_like(raw_scores)
    residual = raw_scores
    direction = raw_scores
    norm_now = total(residual * residual)
    for iteration in range(ITERS):
        image = operator(direction)
        step_size = norm_now / total(direction * image)
        smoothed = smoothed + step_size[None, :, None] * direction
        residual = residual - step_size[None, :, None] * image
        norm_next = total(residual * residual)
        direction = residual + (norm_next / norm_now)[None, :, None] * direction
        norm_now = norm_next
    return smoothed, residual
```

```python
import functools

import jax
import jax.numpy as jnp
from jax import lax
from jax.experimental import pallas as pl
from jax.experimental.pallas import tpu as pltpu
from jax.sharding import PartitionSpec as P

ITERS = 3
MESH = pl.DeviceIdType.MESH
F32 = jnp.float32
BF16 = jnp.bfloat16


def split(x):
    high = x.astype(BF16)
    low = (x - high.astype(F32)).astype(BF16)
    return high, low


def product(field, weights):
    size = field.shape[0]
    width = field.shape[1]
    high, low = split(field)
    both = jnp.concatenate([high, low], axis=0)
    out = jnp.dot(both, weights, preferred_element_type=F32)
    upper = out[:size, :width]
    return upper + ((out[size:, :width] + out[:size, width:]) + out[size:, width:])


def body(
    n_row,
    n_col,
    values_hbm,
    order,
    keep,
    index_ref,
    live_ref,
    gain_ref,
    raw_ref,
    smooth_ref,
    resid_ref,
    *scratch,
):
    names = iter(scratch)
    take = lambda: next(names)
    stored, natural, turned, sums_row, sums_col = take(), take(), take(), take(), take()
    running, row_part, col_part = take(), take(), take()
    resid, degree, direct, image = take(), take(), take(), take()
    panel_rows = [take() for _ in range(ITERS)]
    panel_cols = [take() for _ in range(ITERS)]
    row_send = [take() for _ in range(ITERS)]
    col_send = [take() for _ in range(ITERS)]
    row_got = [take() for _ in range(ITERS)]
    col_got = [take() for _ in range(ITERS)]
    dot_own = [take() for _ in range(ITERS)]
    dot_line = [take() for _ in range(ITERS)]
    dot_col_got = [take() for _ in range(ITERS)]
    dot_row_got = [take() for _ in range(ITERS)]
    deg_row_send, deg_col_send, deg_row_got, deg_col_got = take(), take(), take(), take()
    value_sem = take()
    sent = take()
    got = take()

    a = lax.axis_index("row")
    c = lax.axis_index("col")
    cap = stored.shape[0]
    size = stored.shape[1]
    seg = raw_ref.shape[0]
    rhs = raw_ref.shape[1]
    n_local = n_col * seg
    n_other = n_row * seg

    fetch = pltpu.make_async_copy(values_hbm.at[0, 0], stored, value_sem)
    fetch.start()

    barrier = pltpu.get_barrier_semaphore()

    def greet_col(k, _):
        pl.semaphore_signal(
            barrier, inc=1, device_id=(a, lax.rem(c + k, n_col)), device_id_type=MESH
        )
        return 0

    def greet_row(k, _):
        pl.semaphore_signal(
            barrier, inc=1, device_id=(lax.rem(a + k, n_row), c), device_id_type=MESH
        )
        return 0

    lax.fori_loop(1, n_col, greet_col, 0)
    lax.fori_loop(1, n_row, greet_row, 0)
    resid[0] = raw_ref[...]
    panel_rows[0][pl.ds(seg * c, seg)] = raw_ref[...]
    panel_cols[0][pl.ds(seg * a, seg)] = raw_ref[...]
    pl.semaphore_wait(barrier, n_col + n_row - 2)

    def along_col(src, dst, peer, which):
        return pltpu.make_async_remote_copy(
            src_ref=src,
            dst_ref=dst,
            send_sem=sent.at[which, peer],
            recv_sem=got.at[which, c],
            device_id=(a, peer),
            device_id_type=MESH,
        )

    def along_row(src, dst, peer, which):
        return pltpu.make_async_remote_copy(
            src_ref=src,
            dst_ref=dst,
            send_sem=sent.at[which, peer],
            recv_sem=got.at[which, a],
            device_id=(peer, c),
            device_id_type=MESH,
        )

    def each_col(act):
        lax.fori_loop(1, n_col, lambda k, _: (act(lax.rem(c + k, n_col)), 0)[1], 0)

    def each_row(act):
        lax.fori_loop(1, n_row, lambda k, _: (act(lax.rem(a + k, n_row)), 0)[1], 0)

    def rows_below(act):
        lax.fori_loop(0, a, lambda k, _: (act(k), 0)[1], 0)

    def rows_above(act):
        lax.fori_loop(a + 1, n_row, lambda k, _: (act(k), 0)[1], 0)

    def arrive(dst, peer, which):
        pltpu.make_async_copy(dst, dst, got.at[which, peer]).wait()

    def leave(src, peer, which):
        pltpu.make_async_copy(src, src, sent.at[which, peer]).wait()

    GATHER_COL, GATHER_ROW, PART_COL, PART_ROW, DOT_COL, DOT_ROW = range(6)
    DEG_COL, DEG_ROW = 6 * ITERS, 6 * ITERS + 1

    def gather(step):
        def to_row(peer):
            along_row(
                resid.at[step],
                panel_cols[step].at[pl.ds(seg * a, seg)],
                peer,
                6 * step + GATHER_ROW,
            ).start()

        def to_col(peer):
            along_col(
                resid.at[step],
                panel_rows[step].at[pl.ds(seg * c, seg)],
                peer,
                6 * step + GATHER_COL,
            ).start()

        rows_below(to_row)
        each_col(to_col)

    gather(0)
    fetch.wait()

    def prepare(q, _):
        block = stored[q]
        flipped = block.T
        high, low = split(block)
        natural[q, :, :size] = high
        natural[q, :, size:] = low
        high, low = split(flipped)
        turned[q, :, :size] = high
        turned[q, :, size:] = low
        sums_row[pl.ds(q, 1), :] = jnp.sum(flipped, axis=0, keepdims=True)
        sums_col[pl.ds(q, 1), :] = jnp.sum(block, axis=0, keepdims=True)
        return 0

    lax.fori_loop(0, cap, prepare, 0, unroll=2)

    live = live_ref[...]

    def pick(line, count):
        wanted = lax.broadcasted_iota(jnp.int32, (count, cap), 0)
        return jnp.where(wanted == index_ref[line : line + 1, :], live, 0.0)

    degree_rows = jnp.dot(
        pick(0, n_local), sums_row[...], precision=lax.Precision.HIGHEST, preferred_element_type=F32
    )
    degree_cols = jnp.dot(
        pick(1, n_other), sums_col[...], precision=lax.Precision.HIGHEST, preferred_element_type=F32
    )
    for peer in range(n_col):
        deg_row_send[peer, 0:seg, :] = degree_rows[seg * peer : seg * peer + seg, :]
    for peer in range(n_row):
        deg_col_send[peer, 0:seg, :] = degree_cols[seg * peer : seg * peer + seg, :]
    each_col(lambda peer: along_col(deg_row_send.at[peer], deg_row_got.at[c], peer, DEG_COL).start())
    rows_above(lambda peer: along_row(deg_col_send.at[peer], deg_col_got.at[a], peer, DEG_ROW).start())
    deg_row_got[c] = deg_row_send[c]
    deg_col_got[a] = deg_col_send[a]

    gains = gain_ref[...]

    def pass_over(weights, panel, base, limit):
        def slot(k, total):
            weight = weights[order[base + k]]
            field = panel[order[base + cap + k]]
            total = total * keep[limit + k] + product(field, weight)
            running[k] = total
            return total

        lax.fori_loop(0, cap, slot, jnp.zeros((rhs, size), F32), unroll=4)

    def total_of(ref, count):
        out = ref[0]
        for k in range(1, count):
            out = out + ref[k]
        return out

    gamma_old = None
    alpha_old = None
    smooth = None
    for step in range(ITERS):
        rows_above(lambda peer: arrive(panel_cols[step].at[pl.ds(seg * peer, seg)], peer, 6 * step + GATHER_ROW))
        pass_over(turned, panel_cols[step], 0, 0)
        for u in range(n_local):
            row_send[step][u] = running[order[4 * cap + u]] * keep[2 * cap + u]
        each_col(
            lambda peer: along_col(
                row_send[step].at[pl.ds(seg * peer, seg)],
                row_got[step].at[pl.ds(seg * c, seg)],
                peer,
                6 * step + PART_COL,
            ).start()
        )
        row_got[step][pl.ds(seg * c, seg)] = row_send[step][pl.ds(seg * c, seg)]
        each_col(lambda peer: arrive(panel_rows[step].at[pl.ds(seg * peer, seg)], peer, 6 * step + GATHER_COL))
        if step == 0:
            each_col(lambda peer: arrive(deg_row_got.at[peer], peer, DEG_COL))
            rows_below(lambda peer: arrive(deg_col_got.at[peer], peer, DEG_ROW))
            here = total_of(deg_row_got, n_col)
            here = here + lax.fori_loop(
                0, a + 1, lambda k, t: t + deg_col_got[k], jnp.zeros_like(here)
            )
            for j in range(seg):
                degree[j] = jnp.broadcast_to(here[j : j + 1, :], (rhs, size))
        own = resid[step]
        square = own * own
        cross = panel_rows[step][0] * row_send[step][0]
        for u in range(1, n_local):
            cross = cross + panel_rows[step][u] * row_send[step][u]
        gamma_part = square[0]
        delta_part = degree[0] * square[0]
        for j in range(1, seg):
            gamma_part = gamma_part + square[j]
            delta_part = delta_part + degree[j] * square[j]
        delta_part = gamma_part + gains * (delta_part - 2.0 * cross)
        parts = jnp.concatenate([gamma_part, delta_part, jnp.zeros((size - 2 * rhs, size), F32)], axis=0)
        summed = jnp.sum(parts.T, axis=0, keepdims=True)
        dot_own[step][...] = jnp.broadcast_to(summed, (8, size))
        each_col(lambda peer: along_col(dot_own[step], dot_col_got[step].at[c], peer, 6 * step + DOT_COL).start())
        dot_col_got[step][c] = dot_own[step][...]

        pass_over(natural, panel_rows[step], 2 * cap, cap)
        for v in range(n_other):
            col_send[step][v] = running[order[4 * cap + n_local + v]] * keep[2 * cap + n_local + v]
        rows_above(
            lambda peer: along_row(
                col_send[step].at[pl.ds(seg * peer, seg)],
                col_got[step].at[pl.ds(seg * a, seg)],
                peer,
                6 * step + PART_ROW,
            ).start()
        )
        col_got[step][pl.ds(seg * a, seg)] = col_send[step][pl.ds(seg * a, seg)]

        each_col(lambda peer: arrive(dot_col_got[step].at[peer], peer, 6 * step + DOT_COL))
        dot_line[step][...] = total_of(dot_col_got[step], n_col)
        each_row(lambda peer: along_row(dot_line[step], dot_row_got[step].at[a], peer, 6 * step + DOT_ROW).start())
        dot_row_got[step][a] = dot_line[step][...]

        each_col(lambda peer: arrive(row_got[step].at[pl.ds(seg * peer, seg)], peer, 6 * step + PART_COL))
        spread = []
        for j in range(seg):
            out = row_got[step][j]
            for k in range(1, n_col):
                out = out + row_got[step][seg * k + j]
            spread.append(out)
        rows_below(lambda peer: arrive(col_got[step].at[pl.ds(seg * peer, seg)], peer, 6 * step + PART_ROW))

        def add_cols(k, both):
            return tuple(both[j] + col_got[step][seg * k + j] for j in range(seg))

        spread = lax.fori_loop(0, a + 1, add_cols, tuple(spread))

        each_row(lambda peer: arrive(dot_row_got[step].at[peer], peer, 6 * step + DOT_ROW))
        dots = total_of(dot_row_got[step], n_row)
        dots = jnp.concatenate([dots] * (size // 8), axis=0).T
        gamma = dots[:rhs, 0:1]
        delta = dots[rhs : 2 * rhs, 0:1]
        if step == 0:
            alpha = gamma / delta
            beta = None
        else:
            beta = gamma / gamma_old
            alpha = gamma / (delta - beta * gamma / alpha_old)
        for j in range(seg):
            r = own[j]
            w = r + gains * (degree[j] * r - spread[j])
            if step == 0:
                d, ad = r, w
                x = alpha * d
            else:
                d = r + beta * direct[j]
                ad = w + beta * image[j]
                x = smooth_ref[j] + alpha * d
            nxt = r - alpha * ad
            smooth_ref[j] = x
            if step < ITERS - 1:
                direct[j] = d
                image[j] = ad
                resid[step + 1, j] = nxt
            else:
                resid_ref[j] = nxt
        if step < ITERS - 1:
            panel_rows[step + 1][pl.ds(seg * c, seg)] = resid[step + 1]
            panel_cols[step + 1][pl.ds(seg * a, seg)] = resid[step + 1]
            gather(step + 1)
        gamma_old, alpha_old = gamma, alpha

    for step in range(ITERS):
        rows_below(lambda peer: leave(resid.at[step], peer, 6 * step + GATHER_ROW))
        each_col(lambda peer: leave(resid.at[step], peer, 6 * step + GATHER_COL))
        each_col(lambda peer: leave(row_send[step].at[pl.ds(seg * peer, seg)], peer, 6 * step + PART_COL))
        rows_above(lambda peer: leave(col_send[step].at[pl.ds(seg * peer, seg)], peer, 6 * step + PART_ROW))
        each_col(lambda peer: leave(dot_own[step], peer, 6 * step + DOT_COL))
        each_row(lambda peer: leave(dot_line[step], peer, 6 * step + DOT_ROW))
    each_col(lambda peer: leave(deg_row_send.at[peer], peer, DEG_COL))
    rows_above(lambda peer: leave(deg_col_send.at[peer], peer, DEG_ROW))


def plan(line, other, count, groups):
    cap = line.shape[0]
    slot = jnp.arange(cap, dtype=jnp.int32)
    live = slot < count
    key = jnp.where(live, line, groups) * cap + slot
    rank = jnp.sum((key[None, :] < key[:, None]).astype(jnp.int32), axis=1)
    at = rank[None, :] == slot[:, None]
    order = jnp.sum(jnp.where(at, slot[None, :], 0), axis=1)
    group = jnp.sum(jnp.where(at, jnp.where(live, line, groups)[None, :], 0), axis=1)
    partner = jnp.sum(jnp.where(at, other[None, :], 0), axis=1)
    order = jnp.where(live, order, order[0])
    partner = jnp.where(live, partner, partner[0])
    follows = jnp.concatenate([jnp.zeros((1,), jnp.int32), (group[1:] == group[:-1]).astype(jnp.int32)])
    below = jnp.sum((jnp.where(live, line, groups)[None, :] <= jnp.arange(groups, dtype=jnp.int32)[:, None]).astype(jnp.int32), axis=1)
    member = jnp.sum((jnp.where(live, line, groups)[None, :] == jnp.arange(groups, dtype=jnp.int32)[:, None]).astype(jnp.int32), axis=1)
    last = jnp.maximum(below - 1, 0)
    return order, partner, follows, last, (member > 0).astype(jnp.int32)


def shards(n_row, n_col, block_values, block_index, block_count, strength, raw_scores):
    cap, size = block_values.shape[2], block_values.shape[3]
    seg, rhs, _ = raw_scores.shape
    rows, cols = block_index[0, 0, 0], block_index[0, 0, 1]
    count = block_count[0, 0]
    n_local, n_other = n_col * seg, n_row * seg
    order_r, partner_r, follows_r, last_r, has_r = plan(rows, cols, count, n_local)
    order_c, partner_c, follows_c, last_c, has_c = plan(cols, rows, count, n_other)
    order = jnp.concatenate([order_r, partner_r, order_c, partner_c, last_r, last_c])
    keep = jnp.concatenate([follows_r, follows_c, has_r, has_c]).astype(F32)
    live = (jnp.arange(cap, dtype=jnp.int32) < count).astype(F32)[None, :]
    gain = jnp.broadcast_to(strength[:, None], (rhs, size))
    field = (seg, rhs, size)
    vmem = pl.BlockSpec(memory_space=pltpu.VMEM)
    smem = pl.BlockSpec(memory_space=pltpu.SMEM)
    many = lambda shape: [pltpu.VMEM(shape, F32) for _ in range(ITERS)]
    scratch = [
        pltpu.VMEM((cap, size, size), F32),
        pltpu.VMEM((cap, size, 2 * size), BF16),
        pltpu.VMEM((cap, size, 2 * size), BF16),
        pltpu.VMEM((cap, size), F32),
        pltpu.VMEM((cap, size), F32),
        pltpu.VMEM((cap, rhs, size), F32),
        pltpu.VMEM((8, size), F32),
        pltpu.VMEM((8, size), F32),
        pltpu.VMEM((ITERS,) + field, F32),
        pltpu.VMEM(field, F32),
        pltpu.VMEM(field, F32),
        pltpu.VMEM(field, F32),
    ]
    scratch += many((n_local, rhs, size)) + many((n_other, rhs, size))
    scratch += many((n_local, rhs, size)) + many((n_other, rhs, size))
    scratch += many((n_local, rhs, size)) + many((n_other, rhs, size))
    scratch += many((8, size)) + many((8, size))
    scratch += many((n_col, 8, size)) + many((n_row, 8, size))
    scratch += [
        pltpu.VMEM((n_col, 8, size), F32),
        pltpu.VMEM((n_row, 8, size), F32),
        pltpu.VMEM((n_col, 8, size), F32),
        pltpu.VMEM((n_row, 8, size), F32),
    ]
    most = max(n_row, n_col)
    scratch += [
        pltpu.SemaphoreType.DMA,
        pltpu.SemaphoreType.DMA((6 * ITERS + 2, most)),
        pltpu.SemaphoreType.DMA((6 * ITERS + 2, most)),
    ]
    return pl.pallas_call(
        functools.partial(body, n_row, n_col),
        out_shape=(jax.ShapeDtypeStruct(field, F32), jax.ShapeDtypeStruct(field, F32)),
        in_specs=[pl.BlockSpec(memory_space=pl.ANY), smem, smem, vmem, vmem, vmem, vmem],
        out_specs=(vmem, vmem),
        scratch_shapes=scratch,
        compiler_params=pltpu.CompilerParams(
            collective_id=0, has_side_effects=True, vmem_limit_bytes=56 * 1024 * 1024
        ),
    )(block_values, order, keep, block_index[0, 0], live, gain, raw_scores)


def solution(mesh):
    n_row, n_col = mesh.shape["row"], mesh.shape["col"]
    placed = (
        P("row", "col", None, None, None),
        P("row", "col", None, None),
        P("row", "col"),
        P(),
        P(("row", "col"), None, None),
    )
    return jax.shard_map(
        functools.partial(shards, n_row, n_col),
        mesh=mesh,
        in_specs=placed,
        out_specs=(P(("row", "col"), None, None), P(("row", "col"), None, None)),
        check_vma=False,
    )
```

```python
import functools

import jax
import jax.numpy as jnp
from jax import lax
from jax.experimental import pallas as pl
from jax.experimental.pallas import tpu as pltpu
from jax.sharding import PartitionSpec as P

ITERS = 3
MESH = pl.DeviceIdType.MESH
F32 = jnp.float32
BF16 = jnp.bfloat16


def split(x):
    high = x.astype(BF16)
    low = (x - high.astype(F32)).astype(BF16)
    return high, low


def product(field, weights):
    size = field.shape[0]
    width = field.shape[1]
    high, low = split(field)
    both = jnp.concatenate([high, low], axis=0)
    out = jnp.dot(both, weights, preferred_element_type=F32)
    upper = out[:size, :width]
    return upper + ((out[size:, :width] + out[:size, width:]) + out[size:, width:])


def body(
    n_row,
    n_col,
    values_hbm,
    order,
    keep,
    index_ref,
    live_ref,
    gain_ref,
    raw_ref,
    smooth_ref,
    resid_ref,
    *scratch,
):
    names = iter(scratch)
    take = lambda: next(names)
    each_step = lambda: [take() for _ in range(ITERS)]
    stored, natural, turned, sums_row, sums_col = take(), take(), take(), take(), take()
    running, resid, degree, direct, image = take(), take(), take(), take(), take()
    panel_rows, panel_cols = each_step(), each_step()
    row_send, col_send = each_step(), each_step()
    swap_got, row_sum = each_step(), each_step()
    row_got, col_got = each_step(), each_step()
    dot_own, dot_line = each_step(), each_step()
    dot_col_got, dot_row_got = each_step(), each_step()
    deg_row_send, deg_col_send, deg_row_got, deg_col_got = take(), take(), take(), take()
    value_sem, sent, got = take(), take(), take()

    a = lax.axis_index("row")
    c = lax.axis_index("col")
    core = lax.rem(c, 2)
    chip = c // 2
    sibling = c + 1 - 2 * core
    n_chip = n_col // 2
    far = sorted(range(1, n_chip), key=lambda k: -min(k, n_chip - k))
    cap = stored.shape[0]
    size = stored.shape[1]
    seg = raw_ref.shape[0]
    rhs = raw_ref.shape[1]
    n_local = n_col * seg
    n_other = n_row * seg
    GATHER_COL, GATHER_ROW, SWAP, PART_COL, PART_ROW, DOT_COL, DOT_ROW = range(7)
    KINDS = 7
    DEG_COL, DEG_ROW = KINDS * ITERS, KINDS * ITERS + 1

    fetch = pltpu.make_async_copy(values_hbm.at[0, 0], stored, value_sem)
    fetch.start()

    barrier = pltpu.get_barrier_semaphore()

    def greet_col(k, _):
        pl.semaphore_signal(
            barrier, inc=1, device_id=(a, lax.rem(c + k, n_col)), device_id_type=MESH
        )
        return 0

    def greet_row(k, _):
        pl.semaphore_signal(
            barrier, inc=1, device_id=(lax.rem(a + k, n_row), c), device_id_type=MESH
        )
        return 0

    lax.fori_loop(1, n_col, greet_col, 0)
    lax.fori_loop(1, n_row, greet_row, 0)
    resid[0] = raw_ref[...]
    panel_rows[0][pl.ds(seg * c, seg)] = raw_ref[...]
    panel_cols[0][pl.ds(seg * a, seg)] = raw_ref[...]
    pl.semaphore_wait(barrier, n_col + n_row - 2)

    def send(src, dst, target, which, out_slot, in_slot):
        pltpu.make_async_remote_copy(
            src_ref=src,
            dst_ref=dst,
            send_sem=sent.at[which, out_slot],
            recv_sem=got.at[which, in_slot],
            device_id=target,
            device_id_type=MESH,
        ).start()

    def each_col(act):
        lax.fori_loop(1, n_col, lambda k, _: (act(lax.rem(c + k, n_col)), 0)[1], 0)

    def each_row(act):
        lax.fori_loop(1, n_row, lambda k, _: (act(lax.rem(a + k, n_row)), 0)[1], 0)

    def rows_below(act):
        lax.fori_loop(0, a, lambda k, _: (act(k), 0)[1], 0)

    def rows_above(act):
        lax.fori_loop(a + 1, n_row, lambda k, _: (act(k), 0)[1], 0)

    def other_chips(act):
        for k in far:
            act(lax.rem(chip + k, n_chip))

    def arrive(dst, which, slot):
        pltpu.make_async_copy(dst, dst, got.at[which, slot]).wait()

    def leave(src, which, slot):
        pltpu.make_async_copy(src, src, sent.at[which, slot]).wait()

    def gather(step):
        where = panel_rows[step].at[pl.ds(seg * c, seg)]
        kind = KINDS * step + GATHER_COL
        other_chips(lambda z: send(resid.at[step], where, (a, 2 * z + core), kind, 0, c))
        send(resid.at[step], where, (a, sibling), kind, 0, c)
        where_col = panel_cols[step].at[pl.ds(seg * a, seg)]
        rows_below(lambda r: send(resid.at[step], where_col, (r, c), kind + GATHER_ROW, r, a))

    def pass_on(step):
        kind = KINDS * step + GATHER_COL
        for k in reversed(far):
            z = lax.rem(chip + k, n_chip)
            piece = panel_rows[step].at[pl.ds(seg * (2 * z + core), seg)]
            arrive(piece, kind, 2 * z + core)
            send(piece, piece, (a, sibling), kind, 1, 2 * z + core)

    def from_sibling(step):
        kind = KINDS * step + GATHER_COL
        for k in [0] + far[::-1]:
            z = lax.rem(chip + k, n_chip)
            slot = 2 * z + 1 - core
            arrive(panel_rows[step].at[pl.ds(seg * slot, seg)], kind, slot)

    def sends_done(step):
        kind = KINDS * step
        some = lambda ref, count: ref.at[pl.ds(0, count)]
        leave(some(panel_rows[step], seg * n_chip), kind + GATHER_COL, 0)
        leave(some(panel_rows[step], seg * (n_chip - 1)), kind + GATHER_COL, 1)
        rows_below(lambda r: leave(resid.at[step], kind + GATHER_ROW, r))
        leave(row_send[step].at[0], kind + SWAP, 0)
        leave(some(row_sum[step], seg * (n_chip - 1)), kind + PART_COL, 0)
        rows_above(lambda r: leave(some(col_send[step], seg), kind + PART_ROW, r))
        leave(some(dot_col_got[step], n_col - 1), kind + DOT_COL, 0)
        leave(some(dot_row_got[step], n_row - 1), kind + DOT_ROW, 0)

    gather(0)
    fetch.wait()

    def prepare(q, _):
        block = stored[q]
        flipped = block.T
        high, low = split(block)
        natural[q, :, :size] = high
        natural[q, :, size:] = low
        high, low = split(flipped)
        turned[q, :, :size] = high
        turned[q, :, size:] = low
        sums_row[pl.ds(q, 1), :] = jnp.sum(flipped, axis=0, keepdims=True)
        sums_col[pl.ds(q, 1), :] = jnp.sum(block, axis=0, keepdims=True)
        return 0

    lax.fori_loop(0, cap, prepare, 0, unroll=2)

    live = live_ref[...]

    def pick(line, count):
        wanted = lax.broadcasted_iota(jnp.int32, (count, cap), 0)
        return jnp.where(wanted == index_ref[line : line + 1, :], live, 0.0)

    degree_rows = jnp.dot(
        pick(0, n_local), sums_row[...], precision=lax.Precision.HIGHEST, preferred_element_type=F32
    )
    degree_cols = jnp.dot(
        pick(1, n_other), sums_col[...], precision=lax.Precision.HIGHEST, preferred_element_type=F32
    )
    for peer in range(n_col):
        deg_row_send[peer] = degree_rows[seg * peer : seg * peer + seg, :]
    for peer in range(n_row):
        deg_col_send[peer] = degree_cols[seg * peer : seg * peer + seg, :]
    each_col(lambda p: send(deg_row_send.at[p], deg_row_got.at[c], (a, p), DEG_COL, 0, 0))
    rows_above(lambda r: send(deg_col_send.at[r], deg_col_got.at[a], (r, c), DEG_ROW, r, a))
    deg_row_got[c] = deg_row_send[c]
    deg_col_got[a] = deg_col_send[a]

    gains = gain_ref[...]

    def pass_over(weights, panel, base, limit):
        def slot(k, total):
            weight = weights[order[base + k]]
            field = panel[order[base + cap + k]]
            total = total * keep[limit + k] + product(field, weight)
            running[k] = total
            return total

        lax.fori_loop(0, cap, slot, jnp.zeros((rhs, size), F32), unroll=4)

    def total_of(ref, count):
        out = ref[0]
        for k in range(1, count):
            out = out + ref[k]
        return out

    def dense_row(c_of):
        return (c_of % 2, (c_of // 2) * seg)

    gamma_old = None
    alpha_old = None
    for step in range(ITERS):
        kind = KINDS * step
        if step > 0:
            sends_done(step - 1)
        rows_above(lambda r: arrive(panel_cols[step].at[pl.ds(seg * r, seg)], kind + GATHER_ROW, r))
        pass_over(turned, panel_cols[step], 0, 0)
        for k in far + [0]:
            z = lax.rem(chip + k, n_chip)
            for half in range(2):
                for j in range(seg):
                    u = seg * (2 * z + half) + j
                    row_send[step][half, seg * z + j] = (
                        running[order[4 * cap + u]] * keep[2 * cap + u]
                    )
            piece = pl.ds(seg * z, seg)
            send(
                row_send[step].at[1 - core, piece],
                swap_got[step].at[piece],
                (a, sibling),
                kind + SWAP,
                0,
                z,
            )
        for k in far + [0]:
            z = lax.rem(chip + k, n_chip)
            piece = pl.ds(seg * z, seg)
            arrive(swap_got[step].at[piece], kind + SWAP, z)
            for j in range(seg):
                row_sum[step][seg * z + j] = row_send[step][core, seg * z + j] + swap_got[step][seg * z + j]
            if k:
                send(
                    row_sum[step].at[piece],
                    row_got[step].at[pl.ds(seg * chip, seg)],
                    (a, 2 * z + core),
                    kind + PART_COL,
                    0,
                    chip,
                )
        pass_on(step)
        from_sibling(step)
        if step == 0:
            arrive(deg_row_got.at[pl.ds(0, n_col - 1)], DEG_COL, 0)
            rows_below(lambda r: arrive(deg_col_got.at[r], DEG_ROW, r))
            here = total_of(deg_row_got, n_col)
            here = here + lax.fori_loop(
                0, a + 1, lambda k, t: t + deg_col_got[k], jnp.zeros_like(here)
            )
            for j in range(seg):
                degree[j] = jnp.broadcast_to(here[j : j + 1, :], (rhs, size))
        own = resid[step]
        square = own * own
        cross = None
        for u in range(n_local):
            half, first = dense_row(u // seg)
            term = panel_rows[step][u] * row_send[step][half, first + u % seg]
            cross = term if cross is None else cross + term
        gamma_part = square[0]
        delta_part = degree[0] * square[0]
        for j in range(1, seg):
            gamma_part = gamma_part + square[j]
            delta_part = delta_part + degree[j] * square[j]
        delta_part = gamma_part + gains * (delta_part - 2.0 * cross)
        parts = jnp.concatenate([gamma_part, delta_part, jnp.zeros((size - 2 * rhs, size), F32)], axis=0)
        dot_own[step][...] = jnp.sum(parts.T, axis=0, keepdims=True)
        each_row(lambda r: send(dot_own[step], dot_row_got[step].at[a], (r, c), kind + DOT_ROW, 0, 0))
        dot_row_got[step][a] = dot_own[step][...]

        pass_over(natural, panel_rows[step], 2 * cap, cap)
        for v in range(n_other):
            col_send[step][v] = running[order[4 * cap + n_local + v]] * keep[2 * cap + n_local + v]
        rows_above(
            lambda r: send(
                col_send[step].at[pl.ds(seg * r, seg)],
                col_got[step].at[pl.ds(seg * a, seg)],
                (r, c),
                kind + PART_ROW,
                r,
                a,
            )
        )
        col_got[step][pl.ds(seg * a, seg)] = col_send[step][pl.ds(seg * a, seg)]

        arrive(dot_row_got[step].at[pl.ds(0, n_row - 1)], kind + DOT_ROW, 0)
        dot_line[step][...] = total_of(dot_row_got[step], n_row)
        each_col(lambda p: send(dot_line[step], dot_col_got[step].at[c], (a, p), kind + DOT_COL, 0, 0))
        dot_col_got[step][c] = dot_line[step][...]

        rows_below(lambda r: arrive(col_got[step].at[pl.ds(seg * r, seg)], kind + PART_ROW, r))

        def add_cols(k, both):
            return tuple(both[j] + col_got[step][seg * k + j] for j in range(seg))

        spread = lax.fori_loop(
            0, a + 1, add_cols, tuple(row_sum[step][seg * chip + j] for j in range(seg))
        )
        spread = list(spread)
        for k in far[::-1]:
            z = lax.rem(chip + k, n_chip)
            arrive(row_got[step].at[pl.ds(seg * z, seg)], kind + PART_COL, z)
            for j in range(seg):
                spread[j] = spread[j] + row_got[step][seg * z + j]

        arrive(dot_col_got[step].at[pl.ds(0, n_col - 1)], kind + DOT_COL, 0)
        dots = total_of(dot_col_got[step], n_col)
        dots = jnp.broadcast_to(dots, (size, size)).T
        gamma = dots[:rhs]
        delta = dots[rhs : 2 * rhs]
        if step == 0:
            alpha = gamma / delta
            beta = None
        else:
            beta = gamma / gamma_old
            alpha = gamma / (delta - beta * gamma / alpha_old)
        for j in range(seg):
            r = own[j]
            w = r + gains * (degree[j] * r - spread[j])
            if step == 0:
                d, ad = r, w
                x = alpha * d
            else:
                d = r + beta * direct[j]
                ad = w + beta * image[j]
                x = smooth_ref[j] + alpha * d
            nxt = r - alpha * ad
            smooth_ref[j] = x
            if step < ITERS - 1:
                direct[j] = d
                image[j] = ad
                resid[step + 1, j] = nxt
            else:
                resid_ref[j] = nxt
        if step < ITERS - 1:
            gather(step + 1)
            panel_rows[step + 1][pl.ds(seg * c, seg)] = resid[step + 1]
            panel_cols[step + 1][pl.ds(seg * a, seg)] = resid[step + 1]
        gamma_old, alpha_old = gamma, alpha

    sends_done(ITERS - 1)
    leave(deg_row_got.at[pl.ds(0, n_col - 1)], DEG_COL, 0)
    rows_above(lambda r: leave(deg_col_send.at[r], DEG_ROW, r))


def plan(line, other, count, groups):
    cap = line.shape[0]
    slot = jnp.arange(cap, dtype=jnp.int32)
    live = slot < count
    key = jnp.where(live, line, groups) * cap + slot
    rank = jnp.sum((key[None, :] < key[:, None]).astype(jnp.int32), axis=1)
    at = rank[None, :] == slot[:, None]
    order = jnp.sum(jnp.where(at, slot[None, :], 0), axis=1)
    group = jnp.sum(jnp.where(at, jnp.where(live, line, groups)[None, :], 0), axis=1)
    partner = jnp.sum(jnp.where(at, other[None, :], 0), axis=1)
    order = jnp.where(live, order, order[0])
    partner = jnp.where(live, partner, partner[0])
    follows = jnp.concatenate([jnp.zeros((1,), jnp.int32), (group[1:] == group[:-1]).astype(jnp.int32)])
    below = jnp.sum((jnp.where(live, line, groups)[None, :] <= jnp.arange(groups, dtype=jnp.int32)[:, None]).astype(jnp.int32), axis=1)
    member = jnp.sum((jnp.where(live, line, groups)[None, :] == jnp.arange(groups, dtype=jnp.int32)[:, None]).astype(jnp.int32), axis=1)
    last = jnp.maximum(below - 1, 0)
    return order, partner, follows, last, (member > 0).astype(jnp.int32)


def shards(n_row, n_col, block_values, block_index, block_count, strength, raw_scores):
    cap, size = block_values.shape[2], block_values.shape[3]
    seg, rhs, _ = raw_scores.shape
    rows, cols = block_index[0, 0, 0], block_index[0, 0, 1]
    count = block_count[0, 0]
    n_local, n_other = n_col * seg, n_row * seg
    order_r, partner_r, follows_r, last_r, has_r = plan(rows, cols, count, n_local)
    order_c, partner_c, follows_c, last_c, has_c = plan(cols, rows, count, n_other)
    order = jnp.concatenate([order_r, partner_r, order_c, partner_c, last_r, last_c])
    keep = jnp.concatenate([follows_r, follows_c, has_r, has_c]).astype(F32)
    live = (jnp.arange(cap, dtype=jnp.int32) < count).astype(F32)[None, :]
    gain = jnp.broadcast_to(strength[:, None], (rhs, size))
    field = (seg, rhs, size)
    vmem = pl.BlockSpec(memory_space=pltpu.VMEM)
    smem = pl.BlockSpec(memory_space=pltpu.SMEM)
    many = lambda shape: [pltpu.VMEM(shape, F32) for _ in range(ITERS)]
    n_chip = n_col // 2
    scratch = [
        pltpu.VMEM((cap, size, size), F32),
        pltpu.VMEM((cap, size, 2 * size), BF16),
        pltpu.VMEM((cap, size, 2 * size), BF16),
        pltpu.VMEM((cap, size), F32),
        pltpu.VMEM((cap, size), F32),
        pltpu.VMEM((cap, rhs, size), F32),
        pltpu.VMEM((ITERS,) + field, F32),
        pltpu.VMEM(field, F32),
        pltpu.VMEM(field, F32),
        pltpu.VMEM(field, F32),
    ]
    scratch += many((n_local, rhs, size)) + many((n_other, rhs, size))
    scratch += many((2, n_chip * seg, rhs, size)) + many((n_other, rhs, size))
    scratch += many((n_chip * seg, rhs, size)) + many((n_chip * seg, rhs, size))
    scratch += many((n_chip * seg, rhs, size)) + many((n_other, rhs, size))
    scratch += many((1, size)) + many((1, size))
    scratch += many((n_col, 1, size)) + many((n_row, 1, size))
    scratch += [
        pltpu.VMEM((n_col, seg, size), F32),
        pltpu.VMEM((n_row, seg, size), F32),
        pltpu.VMEM((n_col, seg, size), F32),
        pltpu.VMEM((n_row, seg, size), F32),
    ]
    most = max(n_row, n_col)
    scratch += [
        pltpu.SemaphoreType.DMA,
        pltpu.SemaphoreType.DMA((7 * ITERS + 2, most)),
        pltpu.SemaphoreType.DMA((7 * ITERS + 2, most)),
    ]
    return pl.pallas_call(
        functools.partial(body, n_row, n_col),
        out_shape=(jax.ShapeDtypeStruct(field, F32), jax.ShapeDtypeStruct(field, F32)),
        in_specs=[pl.BlockSpec(memory_space=pl.ANY), smem, smem, vmem, vmem, vmem, vmem],
        out_specs=(vmem, vmem),
        scratch_shapes=scratch,
        compiler_params=pltpu.CompilerParams(
            collective_id=0, has_side_effects=True, vmem_limit_bytes=56 * 1024 * 1024
        ),
    )(block_values, order, keep, block_index[0, 0], live, gain, raw_scores)


def solution(mesh):
    n_row, n_col = mesh.shape["row"], mesh.shape["col"]
    placed = (
        P("row", "col", None, None, None),
        P("row", "col", None, None),
        P("row", "col"),
        P(),
        P(("row", "col"), None, None),
    )
    return jax.shard_map(
        functools.partial(shards, n_row, n_col),
        mesh=mesh,
        in_specs=placed,
        out_specs=(P(("row", "col"), None, None), P(("row", "col"), None, None)),
        check_vma=False,
    )
```

```python
import functools

import jax
import jax.numpy as jnp
from jax import lax
from jax.experimental import pallas as pl
from jax.experimental.pallas import tpu as pltpu
from jax.sharding import PartitionSpec as P

ITERS = 3
MESH = pl.DeviceIdType.MESH
F32 = jnp.float32
BF16 = jnp.bfloat16


def split(x):
    high = x.astype(BF16)
    low = (x - high.astype(F32)).astype(BF16)
    return high, low


def product(field, weights):
    size = field.shape[0]
    width = field.shape[1]
    high, low = split(field)
    both = jnp.concatenate([high, low], axis=0)
    out = jnp.dot(both, weights, preferred_element_type=F32)
    upper = out[:size, :width]
    return upper + ((out[size:, :width] + out[:size, width:]) + out[size:, width:])


def body(
    n_row,
    n_col,
    values_hbm,
    index_ref,
    count_ref,
    strength_ref,
    raw_ref,
    smooth_ref,
    resid_ref,
    *scratch,
):
    names = iter(scratch)
    take = lambda: next(names)
    each_step = lambda: [take() for _ in range(ITERS)]
    stored, natural, turned, sums_row, sums_col = take(), take(), take(), take(), take()
    running, resid, degree, direct, image = take(), take(), take(), take(), take()
    panel_rows, panel_cols = each_step(), each_step()
    row_send, col_send = each_step(), each_step()
    swap_got, row_sum = each_step(), each_step()
    row_got, col_got = each_step(), each_step()
    dot_own, dot_line = each_step(), each_step()
    dot_col_got, dot_row_got = each_step(), each_step()
    deg_row_send, deg_col_send, deg_row_got, deg_col_got = take(), take(), take(), take()
    gain_ref, listed, slots, scales, slots_at, scales_at = [take() for _ in range(6)]
    value_sem, plan_sem, sent, got = take(), take(), take(), take()

    a = lax.axis_index("row")
    c = lax.axis_index("col")
    core = lax.rem(c, 2)
    chip = c // 2
    sibling = c + 1 - 2 * core
    n_chip = n_col // 2
    far = sorted(range(1, n_chip), key=lambda k: -min(k, n_chip - k))
    cap = stored.shape[0]
    size = stored.shape[1]
    seg = raw_ref.shape[0]
    rhs = raw_ref.shape[1]
    n_local = n_col * seg
    n_other = n_row * seg
    GATHER_COL, GATHER_ROW, SWAP, PART_COL, PART_ROW, DOT_COL, DOT_ROW = range(7)
    KINDS = 7
    DEG_COL, DEG_ROW = KINDS * ITERS, KINDS * ITERS + 1

    fetch = pltpu.make_async_copy(values_hbm.at[0, 0], stored, value_sem)
    fetch.start()

    barrier = pltpu.get_barrier_semaphore()

    def greet_col(k, _):
        pl.semaphore_signal(
            barrier, inc=1, device_id=(a, lax.rem(c + k, n_col)), device_id_type=MESH
        )
        return 0

    def greet_row(k, _):
        pl.semaphore_signal(
            barrier, inc=1, device_id=(lax.rem(a + k, n_row), c), device_id_type=MESH
        )
        return 0

    lax.fori_loop(1, n_col, greet_col, 0)
    lax.fori_loop(1, n_row, greet_row, 0)
    resid[0] = raw_ref[...]
    panel_rows[0][pl.ds(seg * c, seg)] = raw_ref[...]
    panel_cols[0][pl.ds(seg * a, seg)] = raw_ref[...]
    make_plan(index_ref, count_ref[...], cap, n_local, n_other, listed, slots, scales)
    to_slots = pltpu.make_async_copy(slots, slots_at, plan_sem.at[0])
    to_scales = pltpu.make_async_copy(scales, scales_at, plan_sem.at[1])
    to_slots.start()
    to_scales.start()
    for s in range(rhs):
        gain_ref[s : s + 1, :] = jnp.full((1, size), strength_ref[s], F32)
    fetch.wait()

    def prepare(q, _):
        block = stored[q]
        flipped = block.T
        high, low = split(block)
        natural[q, :, :size] = high
        natural[q, :, size:] = low
        high, low = split(flipped)
        turned[q, :, :size] = high
        turned[q, :, size:] = low
        sums_row[pl.ds(q, 1), :] = jnp.sum(flipped, axis=0, keepdims=True)
        sums_col[pl.ds(q, 1), :] = jnp.sum(block, axis=0, keepdims=True)
        return 0

    lax.fori_loop(0, cap // 2, prepare, 0, unroll=2)
    pl.semaphore_wait(barrier, n_col + n_row - 2)

    def send(src, dst, target, which, out_slot, in_slot):
        pltpu.make_async_remote_copy(
            src_ref=src,
            dst_ref=dst,
            send_sem=sent.at[which, out_slot],
            recv_sem=got.at[which, in_slot],
            device_id=target,
            device_id_type=MESH,
        ).start()

    def each_col(act):
        lax.fori_loop(1, n_col, lambda k, _: (act(lax.rem(c + k, n_col)), 0)[1], 0)

    def each_row(act):
        lax.fori_loop(1, n_row, lambda k, _: (act(lax.rem(a + k, n_row)), 0)[1], 0)

    def rows_below(act):
        lax.fori_loop(0, a, lambda k, _: (act(k), 0)[1], 0)

    def rows_above(act):
        lax.fori_loop(a + 1, n_row, lambda k, _: (act(k), 0)[1], 0)

    def other_chips(act):
        for k in far:
            act(lax.rem(chip + k, n_chip))

    def arrive(dst, which, slot):
        pltpu.make_async_copy(dst, dst, got.at[which, slot]).wait()

    def leave(src, which, slot):
        pltpu.make_async_copy(src, src, sent.at[which, slot]).wait()

    def gather(step):
        where = panel_rows[step].at[pl.ds(seg * c, seg)]
        kind = KINDS * step + GATHER_COL
        other_chips(lambda z: send(resid.at[step], where, (a, 2 * z + core), kind, 0, c))
        send(resid.at[step], where, (a, sibling), kind, 0, c)
        where_col = panel_cols[step].at[pl.ds(seg * a, seg)]
        rows_below(lambda r: send(resid.at[step], where_col, (r, c), kind + GATHER_ROW, r, a))

    def pass_on(step):
        kind = KINDS * step + GATHER_COL
        for k in reversed(far):
            z = lax.rem(chip + k, n_chip)
            piece = panel_rows[step].at[pl.ds(seg * (2 * z + core), seg)]
            arrive(piece, kind, 2 * z + core)
            send(piece, piece, (a, sibling), kind, 1, 2 * z + core)

    def from_sibling(step):
        kind = KINDS * step + GATHER_COL
        for k in [0] + far[::-1]:
            z = lax.rem(chip + k, n_chip)
            slot = 2 * z + 1 - core
            arrive(panel_rows[step].at[pl.ds(seg * slot, seg)], kind, slot)

    def sends_done(step):
        kind = KINDS * step
        some = lambda ref, count: ref.at[pl.ds(0, count)]
        leave(some(panel_rows[step], seg * n_chip), kind + GATHER_COL, 0)
        leave(some(panel_rows[step], seg * (n_chip - 1)), kind + GATHER_COL, 1)
        rows_below(lambda r: leave(resid.at[step], kind + GATHER_ROW, r))
        leave(row_send[step].at[0], kind + SWAP, 0)
        leave(some(row_sum[step], seg * (n_chip - 1)), kind + PART_COL, 0)
        rows_above(lambda r: leave(some(col_send[step], seg), kind + PART_ROW, r))
        leave(some(dot_col_got[step], n_col - 1), kind + DOT_COL, 0)
        leave(some(dot_row_got[step], n_row - 1), kind + DOT_ROW, 0)

    gather(0)

    lax.fori_loop(cap // 2, cap, prepare, 0, unroll=2)

    live = lax.broadcasted_iota(jnp.int32, (1, cap), 1) < count_ref[...]

    def pick(line, count):
        wanted = lax.broadcasted_iota(jnp.int32, (count, cap), 0)
        chosen = (wanted == index_ref[0, 0, line : line + 1, :]) & live
        return jnp.where(chosen, 1.0, 0.0)

    degree_rows = jnp.dot(
        pick(0, n_local), sums_row[...], precision=lax.Precision.HIGHEST, preferred_element_type=F32
    )
    degree_cols = jnp.dot(
        pick(1, n_other), sums_col[...], precision=lax.Precision.HIGHEST, preferred_element_type=F32
    )
    for peer in range(n_col):
        deg_row_send[peer] = degree_rows[seg * peer : seg * peer + seg, :]
    for peer in range(n_row):
        deg_col_send[peer] = degree_cols[seg * peer : seg * peer + seg, :]
    each_col(lambda p: send(deg_row_send.at[p], deg_row_got.at[c], (a, p), DEG_COL, 0, 0))
    rows_above(lambda r: send(deg_col_send.at[r], deg_col_got.at[a], (r, c), DEG_ROW, r, a))
    deg_row_got[c] = deg_row_send[c]
    deg_col_got[a] = deg_col_send[a]

    gains = gain_ref[...]
    to_slots.wait()
    to_scales.wait()

    def pass_over(weights, panel, side):
        def slot(k, total):
            weight = weights[slots_at[3 * side, k]]
            field = panel[slots_at[3 * side + 1, k]]
            total = total * scales_at[2 * side, k] + product(field, weight)
            running[k] = total
            return total

        lax.fori_loop(0, cap, slot, jnp.zeros((rhs, size), F32), unroll=4)

    def total_of(ref, count):
        out = ref[0]
        for k in range(1, count):
            out = out + ref[k]
        return out

    def dense_row(c_of):
        return (c_of % 2, (c_of // 2) * seg)

    gamma_old = None
    alpha_old = None
    for step in range(ITERS):
        kind = KINDS * step
        if step > 0:
            sends_done(step - 1)
        rows_above(lambda r: arrive(panel_cols[step].at[pl.ds(seg * r, seg)], kind + GATHER_ROW, r))
        pass_over(turned, panel_cols[step], 0)
        for k in far + [0]:
            z = lax.rem(chip + k, n_chip)
            for half in range(2):
                for j in range(seg):
                    u = seg * (2 * z + half) + j
                    row_send[step][half, seg * z + j] = (
                        running[slots_at[2, u]] * scales_at[1, u]
                    )
            piece = pl.ds(seg * z, seg)
            send(
                row_send[step].at[1 - core, piece],
                swap_got[step].at[piece],
                (a, sibling),
                kind + SWAP,
                0,
                z,
            )
        for k in far + [0]:
            z = lax.rem(chip + k, n_chip)
            piece = pl.ds(seg * z, seg)
            arrive(swap_got[step].at[piece], kind + SWAP, z)
            for j in range(seg):
                row_sum[step][seg * z + j] = row_send[step][core, seg * z + j] + swap_got[step][seg * z + j]
            if k:
                send(
                    row_sum[step].at[piece],
                    row_got[step].at[pl.ds(seg * chip, seg)],
                    (a, 2 * z + core),
                    kind + PART_COL,
                    0,
                    chip,
                )
        pass_on(step)
        from_sibling(step)
        if step == 0:
            arrive(deg_row_got.at[pl.ds(0, n_col - 1)], DEG_COL, 0)
            rows_below(lambda r: arrive(deg_col_got.at[r], DEG_ROW, r))
            here = total_of(deg_row_got, n_col)
            here = here + lax.fori_loop(
                0, a + 1, lambda k, t: t + deg_col_got[k], jnp.zeros_like(here)
            )
            for j in range(seg):
                degree[j] = jnp.broadcast_to(here[j : j + 1, :], (rhs, size))
        own = resid[step]
        square = own * own
        cross = None
        for u in range(n_local):
            half, first = dense_row(u // seg)
            term = panel_rows[step][u] * row_send[step][half, first + u % seg]
            cross = term if cross is None else cross + term
        gamma_part = square[0]
        delta_part = degree[0] * square[0]
        for j in range(1, seg):
            gamma_part = gamma_part + square[j]
            delta_part = delta_part + degree[j] * square[j]
        delta_part = gamma_part + gains * (delta_part - 2.0 * cross)
        parts = jnp.concatenate([gamma_part, delta_part, jnp.zeros((size - 2 * rhs, size), F32)], axis=0)
        dot_own[step][...] = jnp.sum(parts.T, axis=0, keepdims=True)
        each_row(lambda r: send(dot_own[step], dot_row_got[step].at[a], (r, c), kind + DOT_ROW, 0, 0))
        dot_row_got[step][a] = dot_own[step][...]

        pass_over(natural, panel_rows[step], 1)
        for v in range(n_other):
            col_send[step][v] = running[slots_at[5, v]] * scales_at[3, v]
        rows_above(
            lambda r: send(
                col_send[step].at[pl.ds(seg * r, seg)],
                col_got[step].at[pl.ds(seg * a, seg)],
                (r, c),
                kind + PART_ROW,
                r,
                a,
            )
        )
        col_got[step][pl.ds(seg * a, seg)] = col_send[step][pl.ds(seg * a, seg)]

        arrive(dot_row_got[step].at[pl.ds(0, n_row - 1)], kind + DOT_ROW, 0)
        dot_line[step][...] = total_of(dot_row_got[step], n_row)
        each_col(lambda p: send(dot_line[step], dot_col_got[step].at[c], (a, p), kind + DOT_COL, 0, 0))
        dot_col_got[step][c] = dot_line[step][...]

        rows_below(lambda r: arrive(col_got[step].at[pl.ds(seg * r, seg)], kind + PART_ROW, r))

        def add_cols(k, both):
            return tuple(both[j] + col_got[step][seg * k + j] for j in range(seg))

        spread = lax.fori_loop(
            0, a + 1, add_cols, tuple(row_sum[step][seg * chip + j] for j in range(seg))
        )
        spread = list(spread)
        for k in far[::-1]:
            z = lax.rem(chip + k, n_chip)
            arrive(row_got[step].at[pl.ds(seg * z, seg)], kind + PART_COL, z)
            for j in range(seg):
                spread[j] = spread[j] + row_got[step][seg * z + j]

        arrive(dot_col_got[step].at[pl.ds(0, n_col - 1)], kind + DOT_COL, 0)
        dots = total_of(dot_col_got[step], n_col)
        dots = jnp.broadcast_to(dots, (size, size)).T
        gamma = dots[:rhs]
        delta = dots[rhs : 2 * rhs]
        if step == 0:
            alpha = gamma / delta
            beta = None
        else:
            beta = gamma / gamma_old
            alpha = gamma / (delta - beta * gamma / alpha_old)
        for j in range(seg):
            r = own[j]
            w = r + gains * (degree[j] * r - spread[j])
            if step == 0:
                d, ad = r, w
                x = alpha * d
            else:
                d = r + beta * direct[j]
                ad = w + beta * image[j]
                x = smooth_ref[j] + alpha * d
            nxt = r - alpha * ad
            smooth_ref[j] = x
            if step < ITERS - 1:
                direct[j] = d
                image[j] = ad
                resid[step + 1, j] = nxt
            else:
                resid_ref[j] = nxt
        if step < ITERS - 1:
            gather(step + 1)
            panel_rows[step + 1][pl.ds(seg * c, seg)] = resid[step + 1]
            panel_cols[step + 1][pl.ds(seg * a, seg)] = resid[step + 1]
        gamma_old, alpha_old = gamma, alpha

    sends_done(ITERS - 1)
    leave(deg_row_got.at[pl.ds(0, n_col - 1)], DEG_COL, 0)
    rows_above(lambda r: leave(deg_col_send.at[r], DEG_ROW, r))


def make_plan(index_ref, count, cap, n_local, n_other, listed, slots, scales):
    width = listed.shape[1]
    listed[...] = jnp.zeros_like(listed)
    listed[0:2, 0:cap] = index_ref[0, 0]
    down = lax.broadcasted_iota(jnp.int32, (width, width), 0)
    across = lax.broadcasted_iota(jnp.int32, (width, width), 1)
    lines = [jnp.broadcast_to(listed[j : j + 1, :], (width, width)) for j in range(2)]
    turned = [line.T for line in lines]
    for side, groups in enumerate((n_local, n_other)):
        key = jnp.where(across < count, lines[side], groups) * width + across
        group = jnp.where(down < count, turned[side], groups)
        key_down = group * width + down
        rank = jnp.sum(jnp.where(key < key_down, 1, 0), axis=1, keepdims=True)
        at = rank == across
        total = lambda x: jnp.sum(x, axis=0, keepdims=True)
        ordered = total(jnp.where(at, group, 0))
        before = pltpu.roll(ordered, 1, 1)
        first = across[0:1, :] == 0
        below = total(jnp.where(group <= across, 1, 0))
        member = total(jnp.where(group == across, 1, 0))
        slots[3 * side : 3 * side + 1, :] = total(jnp.where(at, down, 0))
        slots[3 * side + 1 : 3 * side + 2, :] = total(jnp.where(at, turned[1 - side], 0))
        slots[3 * side + 2 : 3 * side + 3, :] = jnp.maximum(below - 1, 0)
        scales[2 * side : 2 * side + 1, :] = jnp.where((ordered == before) & ~first, 1.0, 0.0)
        scales[2 * side + 1 : 2 * side + 2, :] = jnp.where(member > 0, 1.0, 0.0)


def shards(n_row, n_col, block_values, block_index, block_count, strength, raw_scores):
    cap, size = block_values.shape[2], block_values.shape[3]
    seg, rhs, _ = raw_scores.shape
    n_local, n_other = n_col * seg, n_row * seg
    field = (seg, rhs, size)
    vmem = pl.BlockSpec(memory_space=pltpu.VMEM)
    smem = pl.BlockSpec(memory_space=pltpu.SMEM)
    many = lambda shape: [pltpu.VMEM(shape, F32) for _ in range(ITERS)]
    n_chip = n_col // 2
    scratch = [
        pltpu.VMEM((cap, size, size), F32),
        pltpu.VMEM((cap, size, 2 * size), BF16),
        pltpu.VMEM((cap, size, 2 * size), BF16),
        pltpu.VMEM((cap, size), F32),
        pltpu.VMEM((cap, size), F32),
        pltpu.VMEM((cap, rhs, size), F32),
        pltpu.VMEM((ITERS,) + field, F32),
        pltpu.VMEM(field, F32),
        pltpu.VMEM(field, F32),
        pltpu.VMEM(field, F32),
    ]
    scratch += many((n_local, rhs, size)) + many((n_other, rhs, size))
    scratch += many((2, n_chip * seg, rhs, size)) + many((n_other, rhs, size))
    scratch += many((n_chip * seg, rhs, size)) + many((n_chip * seg, rhs, size))
    scratch += many((n_chip * seg, rhs, size)) + many((n_other, rhs, size))
    scratch += many((1, size)) + many((1, size))
    scratch += many((n_col, 1, size)) + many((n_row, 1, size))
    scratch += [
        pltpu.VMEM((n_col, seg, size), F32),
        pltpu.VMEM((n_row, seg, size), F32),
        pltpu.VMEM((n_col, seg, size), F32),
        pltpu.VMEM((n_row, seg, size), F32),
    ]
    most = max(n_row, n_col)
    scratch += [
        pltpu.VMEM((rhs, size), F32),
        pltpu.VMEM((8, size), jnp.int32),
        pltpu.VMEM((8, size), jnp.int32),
        pltpu.VMEM((8, size), F32),
        pltpu.SMEM((8, size), jnp.int32),
        pltpu.SMEM((8, size), F32),
        pltpu.SemaphoreType.DMA,
        pltpu.SemaphoreType.DMA((2,)),
        pltpu.SemaphoreType.DMA((7 * ITERS + 2, most)),
        pltpu.SemaphoreType.DMA((7 * ITERS + 2, most)),
    ]
    return pl.pallas_call(
        functools.partial(body, n_row, n_col),
        out_shape=(jax.ShapeDtypeStruct(field, F32), jax.ShapeDtypeStruct(field, F32)),
        in_specs=[pl.BlockSpec(memory_space=pl.ANY), vmem, vmem, smem, vmem],
        out_specs=(vmem, vmem),
        scratch_shapes=scratch,
        compiler_params=pltpu.CompilerParams(
            collective_id=0, has_side_effects=True, vmem_limit_bytes=56 * 1024 * 1024
        ),
    )(block_values, block_index, block_count, strength, raw_scores)


def solution(mesh):
    n_row, n_col = mesh.shape["row"], mesh.shape["col"]
    placed = (
        P("row", "col", None, None, None),
        P("row", "col", None, None),
        P("row", "col"),
        P(),
        P(("row", "col"), None, None),
    )
    return jax.shard_map(
        functools.partial(shards, n_row, n_col),
        mesh=mesh,
        in_specs=placed,
        out_specs=(P(("row", "col"), None, None), P(("row", "col"), None, None)),
        check_vma=False,
    )
```

```python
import functools

import jax
import jax.numpy as jnp
from jax import lax
from jax.experimental import pallas as pl
from jax.experimental.pallas import tpu as pltpu
from jax.sharding import PartitionSpec as P

ITERS = 3
MESH = pl.DeviceIdType.MESH
F32 = jnp.float32
BF16 = jnp.bfloat16


def split(x):
    high = x.astype(BF16)
    low = (x - high.astype(F32)).astype(BF16)
    return high, low


def product(field, weights):
    size = field.shape[0]
    width = field.shape[1]
    high, low = split(field)
    both = jnp.concatenate([high, low], axis=0)
    out = jnp.dot(both, weights, preferred_element_type=F32)
    upper = out[:size, :width]
    return upper + ((out[size:, :width] + out[:size, width:]) + out[size:, width:])


def body(
    n_row,
    n_col,
    values_hbm,
    index_ref,
    count_ref,
    strength_ref,
    raw_ref,
    packed_ref,
    *scratch,
):
    names = iter(scratch)
    smooth_ref, resid_ref = packed_ref.at[0], packed_ref.at[1]
    take = lambda: next(names)
    each_step = lambda: [take() for _ in range(ITERS)]
    stored, natural, turned, sums_row, sums_col = take(), take(), take(), take(), take()
    running, resid, degree, direct, image = take(), take(), take(), take(), take()
    panel_rows, panel_cols = each_step(), each_step()
    row_send, col_send = each_step(), each_step()
    swap_got, row_sum = each_step(), each_step()
    row_got, col_got = each_step(), each_step()
    dot_own, dot_line = each_step(), each_step()
    dot_col_got, dot_row_got = each_step(), each_step()
    deg_row_send, deg_col_send, deg_row_got, deg_col_got = take(), take(), take(), take()
    gain_ref, listed, slots, scales, slots_at, scales_at = [take() for _ in range(6)]
    value_sem, plan_sem, sent, got = take(), take(), take(), take()

    a = lax.axis_index("row")
    c = lax.axis_index("col")
    core = lax.rem(c, 2)
    chip = c // 2
    sibling = c + 1 - 2 * core
    n_chip = n_col // 2
    far = sorted(range(1, n_chip), key=lambda k: -min(k, n_chip - k))
    cap = stored.shape[0]
    size = stored.shape[1]
    seg = raw_ref.shape[0]
    rhs = raw_ref.shape[1]
    n_local = n_col * seg
    n_other = n_row * seg
    GATHER_COL, GATHER_ROW, SWAP, PART_COL, PART_ROW, DOT_COL, DOT_ROW = range(7)
    KINDS = 7
    DEG_COL, DEG_ROW = KINDS * ITERS, KINDS * ITERS + 1

    fetch = pltpu.make_async_copy(values_hbm.at[0, 0], stored, value_sem)
    fetch.start()

    barrier = pltpu.get_barrier_semaphore()

    def greet_col(k, _):
        pl.semaphore_signal(
            barrier, inc=1, device_id=(a, lax.rem(c + k, n_col)), device_id_type=MESH
        )
        return 0

    def greet_row(k, _):
        pl.semaphore_signal(
            barrier, inc=1, device_id=(lax.rem(a + k, n_row), c), device_id_type=MESH
        )
        return 0

    lax.fori_loop(1, n_col, greet_col, 0)
    lax.fori_loop(1, n_row, greet_row, 0)
    resid[0] = raw_ref[...]
    panel_rows[0][pl.ds(seg * c, seg)] = raw_ref[...]
    panel_cols[0][pl.ds(seg * a, seg)] = raw_ref[...]
    make_plan(index_ref, count_ref[...], cap, n_local, n_other, listed, slots, scales)
    to_slots = pltpu.make_async_copy(slots, slots_at, plan_sem.at[0])
    to_scales = pltpu.make_async_copy(scales, scales_at, plan_sem.at[1])
    to_slots.start()
    to_scales.start()
    for s in range(rhs):
        gain_ref[s : s + 1, :] = jnp.full((1, size), strength_ref[s], F32)
    fetch.wait()

    def prepare(q, _):
        block = stored[q]
        flipped = block.T
        high, low = split(block)
        natural[q, :, :size] = high
        natural[q, :, size:] = low
        high, low = split(flipped)
        turned[q, :, :size] = high
        turned[q, :, size:] = low
        sums_row[pl.ds(q, 1), :] = jnp.sum(flipped, axis=0, keepdims=True)
        sums_col[pl.ds(q, 1), :] = jnp.sum(block, axis=0, keepdims=True)
        return 0

    lax.fori_loop(0, cap // 2, prepare, 0, unroll=10)
    pl.semaphore_wait(barrier, n_col + n_row - 2)

    def send(src, dst, target, which, out_slot, in_slot):
        pltpu.make_async_remote_copy(
            src_ref=src,
            dst_ref=dst,
            send_sem=sent.at[which, out_slot],
            recv_sem=got.at[which, in_slot],
            device_id=target,
            device_id_type=MESH,
        ).start()

    def each_col(act):
        lax.fori_loop(1, n_col, lambda k, _: (act(lax.rem(c + k, n_col)), 0)[1], 0)

    def each_row(act):
        lax.fori_loop(1, n_row, lambda k, _: (act(lax.rem(a + k, n_row)), 0)[1], 0)

    def rows_below(act):
        lax.fori_loop(0, a, lambda k, _: (act(k), 0)[1], 0)

    def rows_above(act):
        lax.fori_loop(a + 1, n_row, lambda k, _: (act(k), 0)[1], 0)

    def other_chips(act):
        for k in far:
            act(lax.rem(chip + k, n_chip))

    def arrive(dst, which, slot):
        pltpu.make_async_copy(dst, dst, got.at[which, slot]).wait()

    def leave(src, which, slot):
        pltpu.make_async_copy(src, src, sent.at[which, slot]).wait()

    def gather(step):
        where = panel_rows[step].at[pl.ds(seg * c, seg)]
        kind = KINDS * step + GATHER_COL
        other_chips(lambda z: send(resid.at[step], where, (a, 2 * z + core), kind, 0, c))
        send(resid.at[step], where, (a, sibling), kind, 0, c)
        where_col = panel_cols[step].at[pl.ds(seg * a, seg)]
        rows_below(lambda r: send(resid.at[step], where_col, (r, c), kind + GATHER_ROW, r, a))

    def pass_on(step):
        kind = KINDS * step + GATHER_COL
        for k in reversed(far):
            z = lax.rem(chip + k, n_chip)
            piece = panel_rows[step].at[pl.ds(seg * (2 * z + core), seg)]
            arrive(piece, kind, 2 * z + core)
            send(piece, piece, (a, sibling), kind, 1, 2 * z + core)

    def from_sibling(step):
        kind = KINDS * step + GATHER_COL
        for k in [0] + far[::-1]:
            z = lax.rem(chip + k, n_chip)
            slot = 2 * z + 1 - core
            arrive(panel_rows[step].at[pl.ds(seg * slot, seg)], kind, slot)

    def sends_done(step):
        kind = KINDS * step
        some = lambda ref, count: ref.at[pl.ds(0, count)]
        leave(some(panel_rows[step], seg * n_chip), kind + GATHER_COL, 0)
        leave(some(panel_rows[step], seg * (n_chip - 1)), kind + GATHER_COL, 1)
        rows_below(lambda r: leave(resid.at[step], kind + GATHER_ROW, r))
        leave(row_send[step].at[0], kind + SWAP, 0)
        leave(some(row_sum[step], seg * (n_chip - 1)), kind + PART_COL, 0)
        rows_above(lambda r: leave(some(col_send[step], seg), kind + PART_ROW, r))
        leave(some(dot_col_got[step], n_col - 1), kind + DOT_COL, 0)
        leave(some(dot_row_got[step], n_row - 1), kind + DOT_ROW, 0)

    gather(0)

    lax.fori_loop(cap // 2, cap, prepare, 0, unroll=10)

    live = lax.broadcasted_iota(jnp.int32, (1, cap), 1) < count_ref[...]

    def pick(line, count):
        wanted = lax.broadcasted_iota(jnp.int32, (count, cap), 0)
        chosen = (wanted == index_ref[0, 0, line : line + 1, :]) & live
        return jnp.where(chosen, 1.0, 0.0)

    degree_rows = jnp.dot(
        pick(0, n_local), sums_row[...], precision=lax.Precision.HIGHEST, preferred_element_type=F32
    )
    degree_cols = jnp.dot(
        pick(1, n_other), sums_col[...], precision=lax.Precision.HIGHEST, preferred_element_type=F32
    )
    for peer in range(n_col):
        deg_row_send[peer] = degree_rows[seg * peer : seg * peer + seg, :]
    for peer in range(n_row):
        deg_col_send[peer] = degree_cols[seg * peer : seg * peer + seg, :]
    each_col(lambda p: send(deg_row_send.at[p], deg_row_got.at[c], (a, p), DEG_COL, 0, 0))
    rows_above(lambda r: send(deg_col_send.at[r], deg_col_got.at[a], (r, c), DEG_ROW, r, a))
    deg_row_got[c] = deg_row_send[c]
    deg_col_got[a] = deg_col_send[a]

    gains = gain_ref[...]
    to_slots.wait()
    to_scales.wait()

    def pass_over(weights, panel, side):
        def slot(k, total):
            weight = weights[slots_at[3 * side, k]]
            field = panel[slots_at[3 * side + 1, k]]
            total = total * scales_at[2 * side, k] + product(field, weight)
            running[k] = total
            return total

        lax.fori_loop(0, cap, slot, jnp.zeros((rhs, size), F32), unroll=True)

    def total_of(ref, count):
        out = ref[0]
        for k in range(1, count):
            out = out + ref[k]
        return out

    def dense_row(c_of):
        return (c_of % 2, (c_of // 2) * seg)

    gamma_old = None
    alpha_old = None
    for step in range(ITERS):
        kind = KINDS * step
        if step > 0:
            sends_done(step - 1)
        pass_on(step)
        rows_above(lambda r: arrive(panel_cols[step].at[pl.ds(seg * r, seg)], kind + GATHER_ROW, r))
        pass_over(turned, panel_cols[step], 0)
        for k in far + [0]:
            z = lax.rem(chip + k, n_chip)
            for half in range(2):
                for j in range(seg):
                    u = seg * (2 * z + half) + j
                    row_send[step][half, seg * z + j] = (
                        running[slots_at[2, u]] * scales_at[1, u]
                    )
            piece = pl.ds(seg * z, seg)
            send(
                row_send[step].at[1 - core, piece],
                swap_got[step].at[piece],
                (a, sibling),
                kind + SWAP,
                0,
                z,
            )
        from_sibling(step)
        if step == 0:
            arrive(deg_row_got.at[pl.ds(0, n_col - 1)], DEG_COL, 0)
            rows_below(lambda r: arrive(deg_col_got.at[r], DEG_ROW, r))
            here = total_of(deg_row_got, n_col)
            here = here + lax.fori_loop(
                0, a + 1, lambda k, t: t + deg_col_got[k], jnp.zeros_like(here)
            )
            for j in range(seg):
                degree[j] = jnp.broadcast_to(here[j : j + 1, :], (rhs, size))
        own = resid[step]
        square = own * own
        cross = None
        for u in range(n_local):
            half, first = dense_row(u // seg)
            term = panel_rows[step][u] * row_send[step][half, first + u % seg]
            cross = term if cross is None else cross + term
        gamma_part = square[0]
        delta_part = degree[0] * square[0]
        for j in range(1, seg):
            gamma_part = gamma_part + square[j]
            delta_part = delta_part + degree[j] * square[j]
        delta_part = gamma_part + gains * (delta_part - 2.0 * cross)
        parts = jnp.concatenate([gamma_part, delta_part, jnp.zeros((size - 2 * rhs, size), F32)], axis=0)
        dot_own[step][...] = jnp.sum(parts.T, axis=0, keepdims=True)
        each_row(lambda r: send(dot_own[step], dot_row_got[step].at[a], (r, c), kind + DOT_ROW, 0, 0))
        dot_row_got[step][a] = dot_own[step][...]

        for k in far + [0]:
            z = lax.rem(chip + k, n_chip)
            piece = pl.ds(seg * z, seg)
            arrive(swap_got[step].at[piece], kind + SWAP, z)
            for j in range(seg):
                row_sum[step][seg * z + j] = row_send[step][core, seg * z + j] + swap_got[step][seg * z + j]
            if k:
                send(
                    row_sum[step].at[piece],
                    row_got[step].at[pl.ds(seg * chip, seg)],
                    (a, 2 * z + core),
                    kind + PART_COL,
                    0,
                    chip,
                )
        pass_over(natural, panel_rows[step], 1)
        for v in range(n_other):
            col_send[step][v] = running[slots_at[5, v]] * scales_at[3, v]
        rows_above(
            lambda r: send(
                col_send[step].at[pl.ds(seg * r, seg)],
                col_got[step].at[pl.ds(seg * a, seg)],
                (r, c),
                kind + PART_ROW,
                r,
                a,
            )
        )
        col_got[step][pl.ds(seg * a, seg)] = col_send[step][pl.ds(seg * a, seg)]

        arrive(dot_row_got[step].at[pl.ds(0, n_row - 1)], kind + DOT_ROW, 0)
        dot_line[step][...] = total_of(dot_row_got[step], n_row)
        each_col(lambda p: send(dot_line[step], dot_col_got[step].at[c], (a, p), kind + DOT_COL, 0, 0))
        dot_col_got[step][c] = dot_line[step][...]

        rows_below(lambda r: arrive(col_got[step].at[pl.ds(seg * r, seg)], kind + PART_ROW, r))

        def add_cols(k, both):
            return tuple(both[j] + col_got[step][seg * k + j] for j in range(seg))

        spread = lax.fori_loop(
            0, a + 1, add_cols, tuple(row_sum[step][seg * chip + j] for j in range(seg))
        )
        spread = list(spread)
        for k in far[::-1]:
            z = lax.rem(chip + k, n_chip)
            arrive(row_got[step].at[pl.ds(seg * z, seg)], kind + PART_COL, z)
            for j in range(seg):
                spread[j] = spread[j] + row_got[step][seg * z + j]

        arrive(dot_col_got[step].at[pl.ds(0, n_col - 1)], kind + DOT_COL, 0)
        dots = total_of(dot_col_got[step], n_col)
        dots = jnp.broadcast_to(dots, (size, size)).T
        gamma = dots[:rhs]
        delta = dots[rhs : 2 * rhs]
        if step == 0:
            alpha = gamma / delta
            beta = None
        else:
            beta = gamma / gamma_old
            alpha = gamma / (delta - beta * gamma / alpha_old)
        for j in range(seg):
            r = own[j]
            w = r + gains * (degree[j] * r - spread[j])
            if step == 0:
                d, ad = r, w
                x = alpha * d
            else:
                d = r + beta * direct[j]
                ad = w + beta * image[j]
                x = smooth_ref[j] + alpha * d
            nxt = r - alpha * ad
            smooth_ref[j] = x
            if step < ITERS - 1:
                direct[j] = d
                image[j] = ad
                resid[step + 1, j] = nxt
            else:
                resid_ref[j] = nxt
        if step < ITERS - 1:
            gather(step + 1)
            panel_rows[step + 1][pl.ds(seg * c, seg)] = resid[step + 1]
            panel_cols[step + 1][pl.ds(seg * a, seg)] = resid[step + 1]
        gamma_old, alpha_old = gamma, alpha

    sends_done(ITERS - 1)
    leave(deg_row_got.at[pl.ds(0, n_col - 1)], DEG_COL, 0)
    rows_above(lambda r: leave(deg_col_send.at[r], DEG_ROW, r))


def make_plan(index_ref, count, cap, n_local, n_other, listed, slots, scales):
    width = listed.shape[1]
    listed[...] = jnp.zeros_like(listed)
    listed[0:2, 0:cap] = index_ref[0, 0]
    down = lax.broadcasted_iota(jnp.int32, (width, width), 0)
    across = lax.broadcasted_iota(jnp.int32, (width, width), 1)
    lines = [jnp.broadcast_to(listed[j : j + 1, :], (width, width)) for j in range(2)]
    turned = [line.T for line in lines]
    for side, groups in enumerate((n_local, n_other)):
        key = jnp.where(across < count, lines[side], groups) * width + across
        group = jnp.where(down < count, turned[side], groups)
        key_down = group * width + down
        rank = jnp.sum(jnp.where(key < key_down, 1, 0), axis=1, keepdims=True)
        at = rank == across
        total = lambda x: jnp.sum(x, axis=0, keepdims=True)
        ordered = total(jnp.where(at, group, 0))
        before = pltpu.roll(ordered, 1, 1)
        first = across[0:1, :] == 0
        below = total(jnp.where(group <= across, 1, 0))
        member = total(jnp.where(group == across, 1, 0))
        slots[3 * side : 3 * side + 1, :] = total(jnp.where(at, down, 0))
        slots[3 * side + 1 : 3 * side + 2, :] = total(jnp.where(at, turned[1 - side], 0))
        slots[3 * side + 2 : 3 * side + 3, :] = jnp.maximum(below - 1, 0)
        scales[2 * side : 2 * side + 1, :] = jnp.where((ordered == before) & ~first, 1.0, 0.0)
        scales[2 * side + 1 : 2 * side + 2, :] = jnp.where(member > 0, 1.0, 0.0)


def shards(n_row, n_col, block_values, block_index, block_count, strength, raw_scores):
    cap, size = block_values.shape[2], block_values.shape[3]
    seg, rhs, _ = raw_scores.shape
    n_local, n_other = n_col * seg, n_row * seg
    field = (seg, rhs, size)
    vmem = pl.BlockSpec(memory_space=pltpu.VMEM)
    smem = pl.BlockSpec(memory_space=pltpu.SMEM)
    many = lambda shape: [pltpu.VMEM(shape, F32) for _ in range(ITERS)]
    n_chip = n_col // 2
    scratch = [
        pltpu.VMEM((cap, size, size), F32),
        pltpu.VMEM((cap, size, 2 * size), BF16),
        pltpu.VMEM((cap, size, 2 * size), BF16),
        pltpu.VMEM((cap, size), F32),
        pltpu.VMEM((cap, size), F32),
        pltpu.VMEM((cap, rhs, size), F32),
        pltpu.VMEM((ITERS,) + field, F32),
        pltpu.VMEM(field, F32),
        pltpu.VMEM(field, F32),
        pltpu.VMEM(field, F32),
    ]
    scratch += many((n_local, rhs, size)) + many((n_other, rhs, size))
    scratch += many((2, n_chip * seg, rhs, size)) + many((n_other, rhs, size))
    scratch += many((n_chip * seg, rhs, size)) + many((n_chip * seg, rhs, size))
    scratch += many((n_chip * seg, rhs, size)) + many((n_other, rhs, size))
    scratch += many((1, size)) + many((1, size))
    scratch += many((n_col, 1, size)) + many((n_row, 1, size))
    scratch += [
        pltpu.VMEM((n_col, seg, size), F32),
        pltpu.VMEM((n_row, seg, size), F32),
        pltpu.VMEM((n_col, seg, size), F32),
        pltpu.VMEM((n_row, seg, size), F32),
    ]
    most = max(n_row, n_col)
    scratch += [
        pltpu.VMEM((rhs, size), F32),
        pltpu.VMEM((8, size), jnp.int32),
        pltpu.VMEM((8, size), jnp.int32),
        pltpu.VMEM((8, size), F32),
        pltpu.SMEM((8, size), jnp.int32),
        pltpu.SMEM((8, size), F32),
        pltpu.SemaphoreType.DMA,
        pltpu.SemaphoreType.DMA((2,)),
        pltpu.SemaphoreType.DMA((7 * ITERS + 2, most)),
        pltpu.SemaphoreType.DMA((7 * ITERS + 2, most)),
    ]
    packed = pl.pallas_call(
        functools.partial(body, n_row, n_col),
        out_shape=jax.ShapeDtypeStruct((2,) + field, F32),
        in_specs=[pl.BlockSpec(memory_space=pl.ANY), vmem, vmem, smem, vmem],
        out_specs=vmem,
        scratch_shapes=scratch,
        compiler_params=pltpu.CompilerParams(
            collective_id=0, has_side_effects=True, vmem_limit_bytes=56 * 1024 * 1024
        ),
    )(block_values, block_index, block_count, strength, raw_scores)
    return packed[0], packed[1]


def solution(mesh):
    n_row, n_col = mesh.shape["row"], mesh.shape["col"]
    placed = (
        P("row", "col", None, None, None),
        P("row", "col", None, None),
        P("row", "col"),
        P(),
        P(("row", "col"), None, None),
    )
    return jax.shard_map(
        functools.partial(shards, n_row, n_col),
        mesh=mesh,
        in_specs=placed,
        out_specs=(P(("row", "col"), None, None), P(("row", "col"), None, None)),
        check_vma=False,
    )
```

```python
import functools

import jax
import jax.numpy as jnp
from jax import lax
from jax.experimental import pallas as pl
from jax.experimental.pallas import tpu as pltpu
from jax.sharding import PartitionSpec as P

ITERS = 3
PARTS = 2
MESH = pl.DeviceIdType.MESH
F32 = jnp.float32
BF16 = jnp.bfloat16


def split(x):
    high = x.astype(BF16)
    low = (x - high.astype(F32)).astype(BF16)
    return high, low


def product(field, weights):
    size = field.shape[0]
    width = field.shape[1]
    high, low = split(field)
    both = jnp.concatenate([high, low], axis=0)
    out = jnp.dot(both, weights, preferred_element_type=F32)
    upper = out[:size, :width]
    return upper + ((out[size:, :width] + out[:size, width:]) + out[size:, width:])


def body(
    n_row,
    n_col,
    values_hbm,
    index_ref,
    count_ref,
    strength_ref,
    raw_ref,
    packed_ref,
    *scratch,
):
    names = iter(scratch)
    take = lambda: next(names)
    each_step = lambda: [[take() for _ in range(PARTS)] for _ in range(ITERS)]
    stored, natural, turned, sums_row, sums_col = take(), take(), take(), take(), take()
    degree, direct, smooth = take(), take(), take()
    running = [take() for _ in range(PARTS)]
    got_rows, got_cols = each_step(), each_step()
    res_rows, res_cols = each_step(), each_step()
    row_send, col_send = each_step(), each_step()
    swap_got, row_sum = each_step(), each_step()
    row_got, col_got = each_step(), each_step()
    image = each_step()
    dot_own, dot_line = [take() for _ in range(ITERS)], [take() for _ in range(ITERS)]
    dot_col_got, dot_row_got = [take() for _ in range(ITERS)], [take() for _ in range(ITERS)]
    deg_row_send, deg_col_send, deg_row_got, deg_col_got = take(), take(), take(), take()
    gain_ref, listed, slots, scales, slots_at, scales_at = [take() for _ in range(6)]
    value_sem, plan_sem, sent, got = take(), take(), take(), take()

    a = lax.axis_index("row")
    c = lax.axis_index("col")
    core = lax.rem(c, 2)
    chip = c // 2
    sibling = c + 1 - 2 * core
    n_chip = n_col // 2
    far = sorted(range(1, n_chip), key=lambda k: -min(k, n_chip - k))
    cap = stored.shape[0]
    size = stored.shape[1]
    seg = raw_ref.shape[0]
    rhs = raw_ref.shape[1]
    share = rhs // PARTS
    n_local = n_col * seg
    n_other = n_row * seg
    GATHER_COL, GATHER_ROW, SWAP, PART_COL, PART_ROW = range(5)
    KINDS = 5
    DOTS = KINDS * PARTS * ITERS
    DEG_COL, DEG_ROW = DOTS + 2 * ITERS, DOTS + 2 * ITERS + 1
    sem_row = lambda step, part, kind: (step * PARTS + part) * KINDS + kind
    parts = range(PARTS)
    lanes = lambda part: slice(share * part, share * part + share)

    fetch = pltpu.make_async_copy(values_hbm.at[0, 0], stored, value_sem)
    fetch.start()

    barrier = pltpu.get_barrier_semaphore()

    def greet_col(k, _):
        pl.semaphore_signal(
            barrier, inc=1, device_id=(a, lax.rem(c + k, n_col)), device_id_type=MESH
        )
        return 0

    def greet_row(k, _):
        pl.semaphore_signal(
            barrier, inc=1, device_id=(lax.rem(a + k, n_row), c), device_id_type=MESH
        )
        return 0

    lax.fori_loop(1, n_col, greet_col, 0)
    lax.fori_loop(1, n_row, greet_row, 0)

    def send(src, dst, target, which, out_slot, in_slot):
        pltpu.make_async_remote_copy(
            src_ref=src,
            dst_ref=dst,
            send_sem=sent.at[which, out_slot],
            recv_sem=got.at[which, in_slot],
            device_id=target,
            device_id_type=MESH,
        ).start()

    def each_col(act):
        lax.fori_loop(1, n_col, lambda k, _: (act(lax.rem(c + k, n_col)), 0)[1], 0)

    def each_row(act):
        lax.fori_loop(1, n_row, lambda k, _: (act(lax.rem(a + k, n_row)), 0)[1], 0)

    def rows_below(act):
        lax.fori_loop(0, a, lambda k, _: (act(k), 0)[1], 0)

    def rows_above(act):
        lax.fori_loop(a + 1, n_row, lambda k, _: (act(k), 0)[1], 0)

    def other_chips(act):
        for k in far:
            act(lax.rem(chip + k, n_chip))

    def arrive(dst, which, slot):
        pltpu.make_async_copy(dst, dst, got.at[which, slot]).wait()

    def leave(src, which, slot):
        pltpu.make_async_copy(src, src, sent.at[which, slot]).wait()

    def gather(step, part):
        src = image[step][part]
        kind = sem_row(step, part, GATHER_COL)
        where = got_rows[step][part].at[pl.ds(seg * c, seg)]
        other_chips(lambda z: send(src, where, (a, 2 * z + core), kind, 0, c))
        send(src, where, (a, sibling), kind, 0, c)
        kind = sem_row(step, part, GATHER_ROW)
        where_col = got_cols[step][part].at[pl.ds(seg * a, seg)]
        rows_below(lambda r: send(src, where_col, (r, c), kind, r, a))
        got_rows[step][part][pl.ds(seg * c, seg)] = src[...]
        got_cols[step][part][pl.ds(seg * a, seg)] = src[...]

    def pass_on(step, part):
        kind = sem_row(step, part, GATHER_COL)
        for k in reversed(far):
            z = lax.rem(chip + k, n_chip)
            piece = got_rows[step][part].at[pl.ds(seg * (2 * z + core), seg)]
            arrive(piece, kind, 2 * z + core)
            send(piece, piece, (a, sibling), kind, 1, 2 * z + core)

    def from_sibling(step, part):
        kind = sem_row(step, part, GATHER_COL)
        for k in [0] + far[::-1]:
            z = lax.rem(chip + k, n_chip)
            slot = 2 * z + 1 - core
            arrive(got_rows[step][part].at[pl.ds(seg * slot, seg)], kind, slot)

    def sends_done(step):
        some = lambda ref, count: ref.at[pl.ds(0, count)]
        for part in parts:
            kind = sem_row(step, part, 0)
            leave(some(got_rows[step][part], seg * n_chip), kind + GATHER_COL, 0)
            leave(some(got_rows[step][part], seg * (n_chip - 1)), kind + GATHER_COL, 1)
            rows_below(lambda r: leave(image[step][part], kind + GATHER_ROW, r))
            leave(row_send[step][part].at[0], kind + SWAP, 0)
            leave(some(row_sum[step][part], seg * (n_chip - 1)), kind + PART_COL, 0)
            rows_above(lambda r: leave(some(col_send[step][part], seg), kind + PART_ROW, r))
        leave(some(dot_row_got[step], n_row - 1), DOTS + 2 * step, 0)
        leave(some(dot_col_got[step], n_col - 1), DOTS + 2 * step + 1, 0)

    for part in parts:
        image[0][part][...] = raw_ref[:, lanes(part), :]
    make_plan(index_ref, count_ref[...], cap, n_local, n_other, listed, slots, scales)
    to_slots = pltpu.make_async_copy(slots, slots_at, plan_sem.at[0])
    to_scales = pltpu.make_async_copy(scales, scales_at, plan_sem.at[1])
    to_slots.start()
    to_scales.start()
    for s in range(rhs):
        gain_ref[s : s + 1, :] = jnp.full((1, size), strength_ref[s], F32)
    fetch.wait()

    def prepare(q, _):
        block = stored[q]
        flipped = block.T
        high, low = split(block)
        natural[q, :, :size] = high
        natural[q, :, size:] = low
        high, low = split(flipped)
        turned[q, :, :size] = high
        turned[q, :, size:] = low
        sums_row[pl.ds(q, 1), :] = jnp.sum(flipped, axis=0, keepdims=True)
        sums_col[pl.ds(q, 1), :] = jnp.sum(block, axis=0, keepdims=True)
        return 0

    lax.fori_loop(0, cap // 2, prepare, 0, unroll=10)
    pl.semaphore_wait(barrier, n_col + n_row - 2)
    for part in parts:
        gather(0, part)
    lax.fori_loop(cap // 2, cap, prepare, 0, unroll=10)

    live = lax.broadcasted_iota(jnp.int32, (1, cap), 1) < count_ref[...]

    def pick(line, count):
        wanted = lax.broadcasted_iota(jnp.int32, (count, cap), 0)
        chosen = (wanted == index_ref[0, 0, line : line + 1, :]) & live
        return jnp.where(chosen, 1.0, 0.0)

    degree_rows = jnp.dot(
        pick(0, n_local), sums_row[...], precision=lax.Precision.HIGHEST, preferred_element_type=F32
    )
    degree_cols = jnp.dot(
        pick(1, n_other), sums_col[...], precision=lax.Precision.HIGHEST, preferred_element_type=F32
    )
    for peer in range(n_col):
        deg_row_send[peer] = degree_rows[seg * peer : seg * peer + seg, :]
    for peer in range(n_row):
        deg_col_send[peer] = degree_cols[seg * peer : seg * peer + seg, :]
    each_col(lambda p: send(deg_row_send.at[p], deg_row_got.at[c], (a, p), DEG_COL, 0, 0))
    rows_above(lambda r: send(deg_col_send.at[r], deg_col_got.at[a], (r, c), DEG_ROW, r, a))
    deg_row_got[c] = deg_row_send[c]
    deg_col_got[a] = deg_col_send[a]

    gains = gain_ref[...]
    to_slots.wait()
    to_scales.wait()

    def pass_over(weights, panel, side, out):
        def slot(k, total):
            weight = weights[slots_at[3 * side, k]]
            field = panel[slots_at[3 * side + 1, k]]
            total = total * scales_at[2 * side, k] + product(field, weight)
            out[k] = total
            return total

        lax.fori_loop(0, cap, slot, jnp.zeros((share, size), F32), unroll=True)

    def total_of(ref, count):
        out = ref[0]
        for k in range(1, count):
            out = out + ref[k]
        return out

    alphas, betas, gammas = [], [], []

    def finish_dots(step):
        arrive(dot_col_got[step].at[pl.ds(0, n_col - 1)], DOTS + 2 * step + 1, 0)
        dots = total_of(dot_col_got[step], n_col)
        dots = jnp.broadcast_to(dots, (size, size)).T
        gamma = dots[:rhs]
        delta = dots[rhs : 2 * rhs]
        if step == 0:
            alpha, beta = gamma / delta, None
        else:
            beta = gamma / gammas[-1]
            alpha = gamma / (delta - beta * gamma / alphas[-1])
        alphas.append(alpha)
        betas.append(beta)
        gammas.append(gamma)

    def form(step, part, fetched, formed, count):
        if step == 0:
            return fetched[0][part]
        alpha = alphas[step - 1][lanes(part)]
        before = fetched[0][part] if step == 1 else formed[step - 1][part]
        after = formed[step][part]

        if step == 1:
            def one(k, _):
                after[k] = before[k] - alpha * fetched[1][part][k]
                return 0
        else:
            beta = betas[step - 1][lanes(part)]

            def one(k, _):
                after[k] = before[k] - alpha * (fetched[2][part][k] + beta * fetched[1][part][k])
                return 0

        lax.fori_loop(0, count, one, 0, unroll=8)
        return after

    for step in range(ITERS):
        if step > 0:
            sends_done(step - 1)
            finish_dots(step - 1)
        gamma_part, delta_part, row_panels = [], [], []
        for part in parts:
            kind = sem_row(step, part, 0)
            pass_on(step, part)
            rows_above(lambda r: arrive(got_cols[step][part].at[pl.ds(seg * r, seg)], kind + GATHER_ROW, r))
            panel_cols = form(step, part, got_cols, res_cols, n_other)
            pass_over(turned, panel_cols, 0, running[part])
            for k in far + [0]:
                z = lax.rem(chip + k, n_chip)
                for half in range(2):
                    for j in range(seg):
                        u = seg * (2 * z + half) + j
                        row_send[step][part][half, seg * z + j] = (
                            running[part][slots_at[2, u]] * scales_at[1, u]
                        )
                piece = pl.ds(seg * z, seg)
                send(
                    row_send[step][part].at[1 - core, piece],
                    swap_got[step][part].at[piece],
                    (a, sibling),
                    kind + SWAP,
                    0,
                    z,
                )
            from_sibling(step, part)
            panel_rows = form(step, part, got_rows, res_rows, n_local)
            row_panels.append(panel_rows)
            pass_over(natural, panel_rows, 1, running[part])
            for v in range(n_other):
                col_send[step][part][v] = running[part][slots_at[5, v]] * scales_at[3, v]
            rows_above(
                lambda r: send(
                    col_send[step][part].at[pl.ds(seg * r, seg)],
                    col_got[step][part].at[pl.ds(seg * a, seg)],
                    (r, c),
                    kind + PART_ROW,
                    r,
                    a,
                )
            )
            col_got[step][part][pl.ds(seg * a, seg)] = col_send[step][part][pl.ds(seg * a, seg)]
            if part == PARTS - 1:
                if step == 0:
                    arrive(deg_row_got.at[pl.ds(0, n_col - 1)], DEG_COL, 0)
                    rows_below(lambda r: arrive(deg_col_got.at[r], DEG_ROW, r))
                    here = total_of(deg_row_got, n_col)
                    here = here + lax.fori_loop(
                        0, a + 1, lambda k, t: t + deg_col_got[k], jnp.zeros_like(here)
                    )
                    for j in range(seg):
                        degree[j] = jnp.broadcast_to(here[j : j + 1, :], (share, size))
                for p in parts:
                    cross = None
                    for u in range(n_local):
                        half, first = u // seg % 2, u // seg // 2 * seg
                        term = row_panels[p][u] * row_send[step][p][half, first + u % seg]
                        cross = term if cross is None else cross + term
                    square = [jnp.square(row_panels[p][seg * c + j]) for j in range(seg)]
                    gamma_part.append(functools.reduce(jnp.add, square))
                    rest = functools.reduce(jnp.add, [degree[j] * square[j] for j in range(seg)])
                    delta_part.append(gamma_part[p] + gains[lanes(p)] * (rest - 2.0 * cross))
                stack = jnp.concatenate(
                    gamma_part + delta_part + [jnp.zeros((size - 2 * rhs, size), F32)], axis=0
                )
                dot_own[step][...] = jnp.sum(stack.T, axis=0, keepdims=True)
                each_row(lambda r: send(dot_own[step], dot_row_got[step].at[a], (r, c), DOTS + 2 * step, 0, 0))
                dot_row_got[step][a] = dot_own[step][...]
            for k in far + [0]:
                z = lax.rem(chip + k, n_chip)
                piece = pl.ds(seg * z, seg)
                arrive(swap_got[step][part].at[piece], kind + SWAP, z)
                for j in range(seg):
                    row_sum[step][part][seg * z + j] = (
                        row_send[step][part][core, seg * z + j] + swap_got[step][part][seg * z + j]
                    )
                if k:
                    send(
                        row_sum[step][part].at[piece],
                        row_got[step][part].at[pl.ds(seg * chip, seg)],
                        (a, 2 * z + core),
                        kind + PART_COL,
                        0,
                        chip,
                    )

        fresh = []
        for part in parts:
            kind = sem_row(step, part, 0)
            if part == PARTS - 1:
                arrive(dot_row_got[step].at[pl.ds(0, n_row - 1)], DOTS + 2 * step, 0)
                dot_line[step][...] = total_of(dot_row_got[step], n_row)
                each_col(
                    lambda p: send(
                        dot_line[step], dot_col_got[step].at[c], (a, p), DOTS + 2 * step + 1, 0, 0
                    )
                )
                dot_col_got[step][c] = dot_line[step][...]
            rows_below(lambda r: arrive(col_got[step][part].at[pl.ds(seg * r, seg)], kind + PART_ROW, r))

            def add_cols(k, both):
                return tuple(both[j] + col_got[step][part][seg * k + j] for j in range(seg))

            spread = lax.fori_loop(
                0, a + 1, add_cols, tuple(row_sum[step][part][seg * chip + j] for j in range(seg))
            )
            spread = list(spread)
            for k in far[::-1]:
                z = lax.rem(chip + k, n_chip)
                arrive(row_got[step][part].at[pl.ds(seg * z, seg)], kind + PART_COL, z)
                for j in range(seg):
                    spread[j] = spread[j] + row_got[step][part][seg * z + j]
            w = []
            for j in range(seg):
                r = row_panels[part][seg * c + j]
                w.append(r + gains[lanes(part)] * (degree[j] * r - spread[j]))
            if step < ITERS - 1:
                for j in range(seg):
                    image[step + 1][part][j] = w[j]
                gather(step + 1, part)
            else:
                fresh.append(w)
        if step > 0:
            alpha, beta = alphas[step - 1], betas[step - 1]
            for part in parts:
                for j in range(seg):
                    own = (got_rows[0] if step == 1 else res_rows[step - 1])[part][seg * c + j]
                    if step == 1:
                        direct[j, lanes(part), :] = own
                        smooth[j, lanes(part), :] = alpha[lanes(part)] * own
                    else:
                        d = own + beta[lanes(part)] * direct[j, lanes(part), :]
                        direct[j, lanes(part), :] = d
                        smooth[j, lanes(part), :] = smooth[j, lanes(part), :] + alpha[lanes(part)] * d

    finish_dots(ITERS - 1)
    for part in parts:
        alpha, beta = alphas[-1][lanes(part)], betas[-1][lanes(part)]
        for j in range(seg):
            r = row_panels[part][seg * c + j]
            slope = image[2][part][j] + betas[1][lanes(part)] * image[1][part][j]
            slope = fresh[part][j] + beta * slope
            d = r + beta * direct[j, lanes(part), :]
            packed_ref[0, j, lanes(part), :] = smooth[j, lanes(part), :] + alpha * d
            packed_ref[1, j, lanes(part), :] = r - alpha * slope
    sends_done(ITERS - 1)
    leave(deg_row_got.at[pl.ds(0, n_col - 1)], DEG_COL, 0)
    rows_above(lambda r: leave(deg_col_send.at[r], DEG_ROW, r))


def make_plan(index_ref, count, cap, n_local, n_other, listed, slots, scales):
    width = listed.shape[1]
    listed[...] = jnp.zeros_like(listed)
    listed[0:2, 0:cap] = index_ref[0, 0]
    down = lax.broadcasted_iota(jnp.int32, (width, width), 0)
    across = lax.broadcasted_iota(jnp.int32, (width, width), 1)
    lines = [jnp.broadcast_to(listed[j : j + 1, :], (width, width)) for j in range(2)]
    turned = [line.T for line in lines]
    for side, groups in enumerate((n_local, n_other)):
        key = jnp.where(across < count, lines[side], groups) * width + across
        group = jnp.where(down < count, turned[side], groups)
        key_down = group * width + down
        rank = jnp.sum(jnp.where(key < key_down, 1, 0), axis=1, keepdims=True)
        at = rank == across
        total = lambda x: jnp.sum(x, axis=0, keepdims=True)
        ordered = total(jnp.where(at, group, 0))
        before = pltpu.roll(ordered, 1, 1)
        first = across[0:1, :] == 0
        below = total(jnp.where(group <= across, 1, 0))
        member = total(jnp.where(group == across, 1, 0))
        slots[3 * side : 3 * side + 1, :] = total(jnp.where(at, down, 0))
        slots[3 * side + 1 : 3 * side + 2, :] = total(jnp.where(at, turned[1 - side], 0))
        slots[3 * side + 2 : 3 * side + 3, :] = jnp.maximum(below - 1, 0)
        scales[2 * side : 2 * side + 1, :] = jnp.where((ordered == before) & ~first, 1.0, 0.0)
        scales[2 * side + 1 : 2 * side + 2, :] = jnp.where(member > 0, 1.0, 0.0)


def shards(n_row, n_col, block_values, block_index, block_count, strength, raw_scores):
    cap, size = block_values.shape[2], block_values.shape[3]
    seg, rhs, _ = raw_scores.shape
    n_local, n_other = n_col * seg, n_row * seg
    field = (seg, rhs, size)
    vmem = pl.BlockSpec(memory_space=pltpu.VMEM)
    smem = pl.BlockSpec(memory_space=pltpu.SMEM)
    n_chip = n_col // 2
    share = rhs // PARTS
    whole = lambda shape: [pltpu.VMEM(shape, F32)]
    many = lambda count: [pltpu.VMEM((count, share, size), F32) for _ in range(ITERS * PARTS)]
    scratch = [
        pltpu.VMEM((cap, size, size), F32),
        pltpu.VMEM((cap, size, 2 * size), BF16),
        pltpu.VMEM((cap, size, 2 * size), BF16),
        pltpu.VMEM((cap, size), F32),
        pltpu.VMEM((cap, size), F32),
        pltpu.VMEM((seg, share, size), F32),
        pltpu.VMEM(field, F32),
        pltpu.VMEM(field, F32),
    ]
    scratch += whole((cap, share, size)) * PARTS
    scratch += many(n_local) + many(n_other)
    scratch += many(n_local) + many(n_other)
    scratch += whole((2, n_chip * seg, share, size)) * (ITERS * PARTS) + many(n_other)
    scratch += many(n_chip * seg) + many(n_chip * seg)
    scratch += many(n_chip * seg) + many(n_other)
    scratch += many(seg)
    scratch += whole((1, size)) * (2 * ITERS)
    scratch += whole((n_col, 1, size)) * ITERS + whole((n_row, 1, size)) * ITERS
    scratch += [
        pltpu.VMEM((n_col, seg, size), F32),
        pltpu.VMEM((n_row, seg, size), F32),
        pltpu.VMEM((n_col, seg, size), F32),
        pltpu.VMEM((n_row, seg, size), F32),
    ]
    most = max(n_row, n_col)
    rows = 5 * PARTS * ITERS + 2 * ITERS + 2
    scratch += [
        pltpu.VMEM((rhs, size), F32),
        pltpu.VMEM((8, size), jnp.int32),
        pltpu.VMEM((8, size), jnp.int32),
        pltpu.VMEM((8, size), F32),
        pltpu.SMEM((8, size), jnp.int32),
        pltpu.SMEM((8, size), F32),
        pltpu.SemaphoreType.DMA,
        pltpu.SemaphoreType.DMA((2,)),
        pltpu.SemaphoreType.DMA((rows, most)),
        pltpu.SemaphoreType.DMA((rows, most)),
    ]
    packed = pl.pallas_call(
        functools.partial(body, n_row, n_col),
        out_shape=jax.ShapeDtypeStruct((2,) + field, F32),
        in_specs=[pl.BlockSpec(memory_space=pl.ANY), vmem, vmem, smem, vmem],
        out_specs=vmem,
        scratch_shapes=scratch,
        compiler_params=pltpu.CompilerParams(
            collective_id=0, has_side_effects=True, vmem_limit_bytes=56 * 1024 * 1024
        ),
    )(block_values, block_index, block_count, strength, raw_scores)
    return packed[0], packed[1]


def solution(mesh):
    n_row, n_col = mesh.shape["row"], mesh.shape["col"]
    placed = (
        P("row", "col", None, None, None),
        P("row", "col", None, None),
        P("row", "col"),
        P(),
        P(("row", "col"), None, None),
    )
    return jax.shard_map(
        functools.partial(shards, n_row, n_col),
        mesh=mesh,
        in_specs=placed,
        out_specs=(P(("row", "col"), None, None), P(("row", "col"), None, None)),
        check_vma=False,
    )
```

```python
import functools

import jax
import jax.numpy as jnp
from jax import lax
from jax.experimental import pallas as pl
from jax.experimental.pallas import tpu as pltpu
from jax.sharding import PartitionSpec as P

ITERS = 3
PARTS = 2
MESH = pl.DeviceIdType.MESH
F32 = jnp.float32
BF16 = jnp.bfloat16


def split(x):
    high = x.astype(BF16)
    low = (x - high.astype(F32)).astype(BF16)
    return high, low


def product(field, weights):
    size = field.shape[0]
    width = field.shape[1]
    high, low = split(field)
    both = jnp.concatenate([high, low], axis=0)
    out = jnp.dot(both, weights, preferred_element_type=F32)
    upper = out[:size, :width]
    return upper + ((out[size:, :width] + out[:size, width:]) + out[size:, width:])


def body(
    n_row,
    n_col,
    values_hbm,
    index_ref,
    count_ref,
    strength_ref,
    raw_ref,
    packed_ref,
    *scratch,
):
    names = iter(scratch)
    take = lambda: next(names)
    each_step = lambda: [[take() for _ in range(PARTS)] for _ in range(ITERS)]
    stored, natural, turned, sums_row, sums_col = take(), take(), take(), take(), take()
    degree, direct, smooth = take(), take(), take()
    running = [take() for _ in range(PARTS)]
    got_rows, got_cols = each_step(), each_step()
    res_rows, res_cols = each_step(), each_step()
    row_send, col_send = each_step(), each_step()
    swap_got, row_sum = each_step(), each_step()
    row_got, col_got = each_step(), each_step()
    image = each_step()
    dot_own, dot_line = [take() for _ in range(ITERS)], [take() for _ in range(ITERS)]
    dot_col_got, dot_row_got = [take() for _ in range(ITERS)], [take() for _ in range(ITERS)]
    deg_row_send, deg_col_send, deg_row_got, deg_col_got = take(), take(), take(), take()
    gain_ref, listed, slots, scales, slots_at, scales_at = [take() for _ in range(6)]
    value_sem, plan_sem, sent, got = take(), take(), take(), take()

    a = lax.axis_index("row")
    c = lax.axis_index("col")
    core = lax.rem(c, 2)
    chip = c // 2
    sibling = c + 1 - 2 * core
    n_chip = n_col // 2
    far = sorted(range(1, n_chip), key=lambda k: -min(k, n_chip - k))
    cap = stored.shape[0]
    size = stored.shape[1]
    seg = raw_ref.shape[0]
    rhs = raw_ref.shape[1]
    share = rhs // PARTS
    n_local = n_col * seg
    n_other = n_row * seg
    GATHER_COL, GATHER_ROW, SWAP, PART_COL, PART_ROW = range(5)
    KINDS = 5
    DOTS = KINDS * PARTS * ITERS
    DEG_COL, DEG_ROW = DOTS + 2 * ITERS, DOTS + 2 * ITERS + 1
    sem_row = lambda step, part, kind: (step * PARTS + part) * KINDS + kind
    parts = range(PARTS)
    lanes = lambda part: slice(share * part, share * part + share)

    fetch = pltpu.make_async_copy(values_hbm.at[0, 0], stored, value_sem)
    fetch.start()

    barrier = pltpu.get_barrier_semaphore()

    def greet_col(k, _):
        pl.semaphore_signal(
            barrier, inc=1, device_id=(a, lax.rem(c + k, n_col)), device_id_type=MESH
        )
        return 0

    def greet_row(k, _):
        pl.semaphore_signal(
            barrier, inc=1, device_id=(lax.rem(a + k, n_row), c), device_id_type=MESH
        )
        return 0

    lax.fori_loop(1, n_col, greet_col, 0)
    lax.fori_loop(1, n_row, greet_row, 0)

    def send(src, dst, target, which, out_slot, in_slot):
        pltpu.make_async_remote_copy(
            src_ref=src,
            dst_ref=dst,
            send_sem=sent.at[which, out_slot],
            recv_sem=got.at[which, in_slot],
            device_id=target,
            device_id_type=MESH,
        ).start()

    def each_col(act):
        lax.fori_loop(1, n_col, lambda k, _: (act(lax.rem(c + k, n_col)), 0)[1], 0)

    def each_row(act):
        lax.fori_loop(1, n_row, lambda k, _: (act(lax.rem(a + k, n_row)), 0)[1], 0)

    def rows_below(act):
        lax.fori_loop(0, a, lambda k, _: (act(k), 0)[1], 0)

    def rows_above(act):
        lax.fori_loop(a + 1, n_row, lambda k, _: (act(k), 0)[1], 0)

    def other_chips(act):
        for k in far:
            act(lax.rem(chip + k, n_chip))

    def arrive(dst, which, slot):
        pltpu.make_async_copy(dst, dst, got.at[which, slot]).wait()

    def leave(src, which, slot):
        pltpu.make_async_copy(src, src, sent.at[which, slot]).wait()

    def gather(step, part):
        src = image[step][part]
        kind = sem_row(step, part, GATHER_COL)
        where = got_rows[step][part].at[pl.ds(seg * c, seg)]
        other_chips(lambda z: send(src, where, (a, 2 * z + core), kind, 0, c))
        send(src, where, (a, sibling), kind, 0, c)
        kind = sem_row(step, part, GATHER_ROW)
        where_col = got_cols[step][part].at[pl.ds(seg * a, seg)]
        rows_below(lambda r: send(src, where_col, (r, c), kind, r, a))
        got_rows[step][part][pl.ds(seg * c, seg)] = src[...]
        got_cols[step][part][pl.ds(seg * a, seg)] = src[...]

    def pass_on(step, part):
        kind = sem_row(step, part, GATHER_COL)
        for k in reversed(far):
            z = lax.rem(chip + k, n_chip)
            piece = got_rows[step][part].at[pl.ds(seg * (2 * z + core), seg)]
            arrive(piece, kind, 2 * z + core)
            send(piece, piece, (a, sibling), kind, 1, 2 * z + core)

    def from_sibling(step, part):
        kind = sem_row(step, part, GATHER_COL)
        for k in [0] + far[::-1]:
            z = lax.rem(chip + k, n_chip)
            slot = 2 * z + 1 - core
            arrive(got_rows[step][part].at[pl.ds(seg * slot, seg)], kind, slot)

    def sends_done(step):
        some = lambda ref, count: ref.at[pl.ds(0, count)]
        for part in parts:
            kind = sem_row(step, part, 0)
            leave(some(got_rows[step][part], seg * n_chip), kind + GATHER_COL, 0)
            leave(some(got_rows[step][part], seg * (n_chip - 1)), kind + GATHER_COL, 1)
            rows_below(lambda r: leave(image[step][part], kind + GATHER_ROW, r))
            leave(row_send[step][part].at[0], kind + SWAP, 0)
            leave(some(row_sum[step][part], seg * (n_chip - 1)), kind + PART_COL, 0)
            rows_above(lambda r: leave(some(col_send[step][part], seg), kind + PART_ROW, r))
        leave(some(dot_col_got[step], n_col - 1), DOTS + 2 * step, 0)
        leave(some(dot_row_got[step], n_row - 1), DOTS + 2 * step + 1, 0)

    for part in parts:
        image[0][part][...] = raw_ref[:, lanes(part), :]
    make_plan(index_ref, count_ref[...], cap, n_local, n_other, listed, slots, scales)
    to_slots = pltpu.make_async_copy(slots, slots_at, plan_sem.at[0])
    to_scales = pltpu.make_async_copy(scales, scales_at, plan_sem.at[1])
    to_slots.start()
    to_scales.start()
    for s in range(rhs):
        gain_ref[s : s + 1, :] = jnp.full((1, size), strength_ref[s], F32)
    fetch.wait()

    def prepare(q, _):
        block = stored[q]
        flipped = block.T
        high, low = split(block)
        natural[q, :, :size] = high
        natural[q, :, size:] = low
        high, low = split(flipped)
        turned[q, :, :size] = high
        turned[q, :, size:] = low
        sums_row[pl.ds(q, 1), :] = jnp.sum(flipped, axis=0, keepdims=True)
        sums_col[pl.ds(q, 1), :] = jnp.sum(block, axis=0, keepdims=True)
        return 0

    lax.fori_loop(0, cap // 2, prepare, 0, unroll=10)
    pl.semaphore_wait(barrier, n_col + n_row - 2)
    for part in parts:
        gather(0, part)
    lax.fori_loop(cap // 2, cap, prepare, 0, unroll=10)

    live = lax.broadcasted_iota(jnp.int32, (1, cap), 1) < count_ref[...]

    def pick(line, count):
        wanted = lax.broadcasted_iota(jnp.int32, (count, cap), 0)
        chosen = (wanted == index_ref[0, 0, line : line + 1, :]) & live
        return jnp.where(chosen, 1.0, 0.0)

    degree_rows = jnp.dot(
        pick(0, n_local), sums_row[...], precision=lax.Precision.HIGHEST, preferred_element_type=F32
    )
    degree_cols = jnp.dot(
        pick(1, n_other), sums_col[...], precision=lax.Precision.HIGHEST, preferred_element_type=F32
    )
    for peer in range(n_col):
        deg_row_send[peer] = degree_rows[seg * peer : seg * peer + seg, :]
    for peer in range(n_row):
        deg_col_send[peer] = degree_cols[seg * peer : seg * peer + seg, :]
    each_col(lambda p: send(deg_row_send.at[p], deg_row_got.at[c], (a, p), DEG_COL, 0, 0))
    rows_above(lambda r: send(deg_col_send.at[r], deg_col_got.at[a], (r, c), DEG_ROW, r, a))
    deg_row_got[c] = deg_row_send[c]
    deg_col_got[a] = deg_col_send[a]

    gains = gain_ref[...]
    to_slots.wait()
    to_scales.wait()

    def pass_over(weights, panel, side, out):
        def slot(k, total):
            weight = weights[slots_at[3 * side, k]]
            field = panel[slots_at[3 * side + 1, k]]
            total = total * scales_at[2 * side, k] + product(field, weight)
            out[k] = total
            return total

        lax.fori_loop(0, cap, slot, jnp.zeros((share, size), F32), unroll=True)

    def total_of(ref, count):
        out = ref[0]
        for k in range(1, count):
            out = out + ref[k]
        return out

    alphas, betas, gammas = [], [], []

    def finish_dots(step):
        arrive(dot_row_got[step].at[pl.ds(0, n_row - 1)], DOTS + 2 * step + 1, 0)
        dots = total_of(dot_row_got[step], n_row)
        dots = jnp.broadcast_to(dots, (size, size)).T
        gamma = dots[:rhs]
        delta = dots[rhs : 2 * rhs]
        if step == 0:
            alpha, beta = gamma / delta, None
        else:
            beta = gamma / gammas[-1]
            alpha = gamma / (delta - beta * gamma / alphas[-1])
        alphas.append(alpha)
        betas.append(beta)
        gammas.append(gamma)

    def form(step, part, fetched, formed, count):
        if step == 0:
            return fetched[0][part]
        alpha = alphas[step - 1][lanes(part)]
        before = fetched[0][part] if step == 1 else formed[step - 1][part]
        after = formed[step][part]

        if step == 1:
            def one(k, _):
                after[k] = before[k] - alpha * fetched[1][part][k]
                return 0
        else:
            beta = betas[step - 1][lanes(part)]

            def one(k, _):
                after[k] = before[k] - alpha * (fetched[2][part][k] + beta * fetched[1][part][k])
                return 0

        lax.fori_loop(0, count, one, 0, unroll=8)
        return after

    for step in range(ITERS):
        if step > 0:
            sends_done(step - 1)
            finish_dots(step - 1)
        gamma_part, delta_part, row_panels = [], [], []
        for part in parts:
            kind = sem_row(step, part, 0)
            pass_on(step, part)
            rows_above(lambda r: arrive(got_cols[step][part].at[pl.ds(seg * r, seg)], kind + GATHER_ROW, r))
            panel_cols = form(step, part, got_cols, res_cols, n_other)
            pass_over(turned, panel_cols, 0, running[part])
            for k in far + [0]:
                z = lax.rem(chip + k, n_chip)
                for half in range(2):
                    for j in range(seg):
                        u = seg * (2 * z + half) + j
                        row_send[step][part][half, seg * z + j] = (
                            running[part][slots_at[2, u]] * scales_at[1, u]
                        )
                piece = pl.ds(seg * z, seg)
                send(
                    row_send[step][part].at[1 - core, piece],
                    swap_got[step][part].at[piece],
                    (a, sibling),
                    kind + SWAP,
                    0,
                    z,
                )
            from_sibling(step, part)
            panel_rows = form(step, part, got_rows, res_rows, n_local)
            row_panels.append(panel_rows)
            pass_over(natural, panel_rows, 1, running[part])
            for v in range(n_other):
                col_send[step][part][v] = running[part][slots_at[5, v]] * scales_at[3, v]
            rows_above(
                lambda r: send(
                    col_send[step][part].at[pl.ds(seg * r, seg)],
                    col_got[step][part].at[pl.ds(seg * a, seg)],
                    (r, c),
                    kind + PART_ROW,
                    r,
                    a,
                )
            )
            col_got[step][part][pl.ds(seg * a, seg)] = col_send[step][part][pl.ds(seg * a, seg)]
            if part == PARTS - 1:
                if step == 0:
                    arrive(deg_row_got.at[pl.ds(0, n_col - 1)], DEG_COL, 0)
                    rows_below(lambda r: arrive(deg_col_got.at[r], DEG_ROW, r))
                    here = total_of(deg_row_got, n_col)
                    here = here + lax.fori_loop(
                        0, a + 1, lambda k, t: t + deg_col_got[k], jnp.zeros_like(here)
                    )
                    for j in range(seg):
                        degree[j] = jnp.broadcast_to(here[j : j + 1, :], (share, size))
                for p in parts:
                    cross = None
                    for u in range(n_local):
                        half, first = u // seg % 2, u // seg // 2 * seg
                        term = row_panels[p][u] * row_send[step][p][half, first + u % seg]
                        cross = term if cross is None else cross + term
                    square = [jnp.square(row_panels[p][seg * c + j]) for j in range(seg)]
                    gamma_part.append(functools.reduce(jnp.add, square))
                    rest = functools.reduce(jnp.add, [degree[j] * square[j] for j in range(seg)])
                    delta_part.append(gamma_part[p] + gains[lanes(p)] * (rest - 2.0 * cross))
                stack = jnp.concatenate(
                    gamma_part + delta_part + [jnp.zeros((size - 2 * rhs, size), F32)], axis=0
                )
                dot_own[step][...] = jnp.sum(stack.T, axis=0, keepdims=True)
                each_col(lambda p: send(dot_own[step], dot_col_got[step].at[c], (a, p), DOTS + 2 * step, 0, 0))
                dot_col_got[step][c] = dot_own[step][...]
            for k in far + [0]:
                z = lax.rem(chip + k, n_chip)
                piece = pl.ds(seg * z, seg)
                arrive(swap_got[step][part].at[piece], kind + SWAP, z)
                for j in range(seg):
                    row_sum[step][part][seg * z + j] = (
                        row_send[step][part][core, seg * z + j] + swap_got[step][part][seg * z + j]
                    )
                if k:
                    send(
                        row_sum[step][part].at[piece],
                        row_got[step][part].at[pl.ds(seg * chip, seg)],
                        (a, 2 * z + core),
                        kind + PART_COL,
                        0,
                        chip,
                    )

        fresh = []
        for part in parts:
            kind = sem_row(step, part, 0)
            if part == PARTS - 1:
                arrive(dot_col_got[step].at[pl.ds(0, n_col - 1)], DOTS + 2 * step, 0)
                dot_line[step][...] = total_of(dot_col_got[step], n_col)
                each_row(
                    lambda r: send(
                        dot_line[step], dot_row_got[step].at[a], (r, c), DOTS + 2 * step + 1, 0, 0
                    )
                )
                dot_row_got[step][a] = dot_line[step][...]
            rows_below(lambda r: arrive(col_got[step][part].at[pl.ds(seg * r, seg)], kind + PART_ROW, r))

            def add_cols(k, both):
                return tuple(both[j] + col_got[step][part][seg * k + j] for j in range(seg))

            spread = lax.fori_loop(
                0, a + 1, add_cols, tuple(row_sum[step][part][seg * chip + j] for j in range(seg))
            )
            spread = list(spread)
            for k in far[::-1]:
                z = lax.rem(chip + k, n_chip)
                arrive(row_got[step][part].at[pl.ds(seg * z, seg)], kind + PART_COL, z)
                for j in range(seg):
                    spread[j] = spread[j] + row_got[step][part][seg * z + j]
            w = []
            for j in range(seg):
                r = row_panels[part][seg * c + j]
                w.append(r + gains[lanes(part)] * (degree[j] * r - spread[j]))
            if step < ITERS - 1:
                for j in range(seg):
                    image[step + 1][part][j] = w[j]
                gather(step + 1, part)
            else:
                fresh.append(w)
        if step > 0:
            alpha, beta = alphas[step - 1], betas[step - 1]
            for part in parts:
                for j in range(seg):
                    own = (got_rows[0] if step == 1 else res_rows[step - 1])[part][seg * c + j]
                    if step == 1:
                        direct[j, lanes(part), :] = own
                        smooth[j, lanes(part), :] = alpha[lanes(part)] * own
                    else:
                        d = own + beta[lanes(part)] * direct[j, lanes(part), :]
                        direct[j, lanes(part), :] = d
                        smooth[j, lanes(part), :] = smooth[j, lanes(part), :] + alpha[lanes(part)] * d

    sends_done(ITERS - 1)
    leave(deg_row_got.at[pl.ds(0, n_col - 1)], DEG_COL, 0)
    rows_above(lambda r: leave(deg_col_send.at[r], DEG_ROW, r))
    finish_dots(ITERS - 1)
    for part in parts:
        alpha, beta = alphas[-1][lanes(part)], betas[-1][lanes(part)]
        for j in range(seg):
            r = row_panels[part][seg * c + j]
            slope = image[2][part][j] + betas[1][lanes(part)] * image[1][part][j]
            slope = fresh[part][j] + beta * slope
            d = r + beta * direct[j, lanes(part), :]
            packed_ref[0, j, lanes(part), :] = smooth[j, lanes(part), :] + alpha * d
            packed_ref[1, j, lanes(part), :] = r - alpha * slope


def make_plan(index_ref, count, cap, n_local, n_other, listed, slots, scales):
    width = listed.shape[1]
    listed[...] = jnp.zeros_like(listed)
    listed[0:2, 0:cap] = index_ref[0, 0]
    down = lax.broadcasted_iota(jnp.int32, (width, width), 0)
    across = lax.broadcasted_iota(jnp.int32, (width, width), 1)
    lines = [jnp.broadcast_to(listed[j : j + 1, :], (width, width)) for j in range(2)]
    turned = [line.T for line in lines]
    for side, groups in enumerate((n_local, n_other)):
        key = jnp.where(across < count, lines[side], groups) * width + across
        group = jnp.where(down < count, turned[side], groups)
        key_down = group * width + down
        rank = jnp.sum(jnp.where(key < key_down, 1, 0), axis=1, keepdims=True)
        at = rank == across
        total = lambda x: jnp.sum(x, axis=0, keepdims=True)
        ordered = total(jnp.where(at, group, 0))
        before = pltpu.roll(ordered, 1, 1)
        first = across[0:1, :] == 0
        below = total(jnp.where(group <= across, 1, 0))
        member = total(jnp.where(group == across, 1, 0))
        slots[3 * side : 3 * side + 1, :] = total(jnp.where(at, down, 0))
        slots[3 * side + 1 : 3 * side + 2, :] = total(jnp.where(at, turned[1 - side], 0))
        slots[3 * side + 2 : 3 * side + 3, :] = jnp.maximum(below - 1, 0)
        scales[2 * side : 2 * side + 1, :] = jnp.where((ordered == before) & ~first, 1.0, 0.0)
        scales[2 * side + 1 : 2 * side + 2, :] = jnp.where(member > 0, 1.0, 0.0)


def shards(n_row, n_col, block_values, block_index, block_count, strength, raw_scores):
    cap, size = block_values.shape[2], block_values.shape[3]
    seg, rhs, _ = raw_scores.shape
    n_local, n_other = n_col * seg, n_row * seg
    field = (seg, rhs, size)
    vmem = pl.BlockSpec(memory_space=pltpu.VMEM)
    smem = pl.BlockSpec(memory_space=pltpu.SMEM)
    n_chip = n_col // 2
    share = rhs // PARTS
    whole = lambda shape: [pltpu.VMEM(shape, F32)]
    many = lambda count: [pltpu.VMEM((count, share, size), F32) for _ in range(ITERS * PARTS)]
    scratch = [
        pltpu.VMEM((cap, size, size), F32),
        pltpu.VMEM((cap, size, 2 * size), BF16),
        pltpu.VMEM((cap, size, 2 * size), BF16),
        pltpu.VMEM((cap, size), F32),
        pltpu.VMEM((cap, size), F32),
        pltpu.VMEM((seg, share, size), F32),
        pltpu.VMEM(field, F32),
        pltpu.VMEM(field, F32),
    ]
    scratch += whole((cap, share, size)) * PARTS
    scratch += many(n_local) + many(n_other)
    scratch += many(n_local) + many(n_other)
    scratch += whole((2, n_chip * seg, share, size)) * (ITERS * PARTS) + many(n_other)
    scratch += many(n_chip * seg) + many(n_chip * seg)
    scratch += many(n_chip * seg) + many(n_other)
    scratch += many(seg)
    scratch += whole((1, size)) * (2 * ITERS)
    scratch += whole((n_col, 1, size)) * ITERS + whole((n_row, 1, size)) * ITERS
    scratch += [
        pltpu.VMEM((n_col, seg, size), F32),
        pltpu.VMEM((n_row, seg, size), F32),
        pltpu.VMEM((n_col, seg, size), F32),
        pltpu.VMEM((n_row, seg, size), F32),
    ]
    most = max(n_row, n_col)
    rows = 5 * PARTS * ITERS + 2 * ITERS + 2
    scratch += [
        pltpu.VMEM((rhs, size), F32),
        pltpu.VMEM((8, size), jnp.int32),
        pltpu.VMEM((8, size), jnp.int32),
        pltpu.VMEM((8, size), F32),
        pltpu.SMEM((8, size), jnp.int32),
        pltpu.SMEM((8, size), F32),
        pltpu.SemaphoreType.DMA,
        pltpu.SemaphoreType.DMA((2,)),
        pltpu.SemaphoreType.DMA((rows, most)),
        pltpu.SemaphoreType.DMA((rows, most)),
    ]
    packed = pl.pallas_call(
        functools.partial(body, n_row, n_col),
        out_shape=jax.ShapeDtypeStruct((2,) + field, F32),
        in_specs=[pl.BlockSpec(memory_space=pl.ANY), vmem, vmem, smem, vmem],
        out_specs=vmem,
        scratch_shapes=scratch,
        compiler_params=pltpu.CompilerParams(
            collective_id=0, has_side_effects=True, vmem_limit_bytes=56 * 1024 * 1024
        ),
    )(block_values, block_index, block_count, strength, raw_scores)
    return packed[0], packed[1]


def solution(mesh):
    n_row, n_col = mesh.shape["row"], mesh.shape["col"]
    placed = (
        P("row", "col", None, None, None),
        P("row", "col", None, None),
        P("row", "col"),
        P(),
        P(("row", "col"), None, None),
    )
    return jax.shard_map(
        functools.partial(shards, n_row, n_col),
        mesh=mesh,
        in_specs=placed,
        out_specs=(P(("row", "col"), None, None), P(("row", "col"), None, None)),
        check_vma=False,
    )
```

```python
import functools

import jax
import jax.numpy as jnp
from jax import lax
from jax.experimental import pallas as pl
from jax.experimental.pallas import tpu as pltpu
from jax.sharding import PartitionSpec as P

ITERS = 3
PARTS = 2
MESH = pl.DeviceIdType.MESH
F32 = jnp.float32
BF16 = jnp.bfloat16


def split(x):
    high = x.astype(BF16)
    low = (x - high.astype(F32)).astype(BF16)
    return high, low


def product(field, weights):
    size = field.shape[0]
    width = field.shape[1]
    high, low = split(field)
    both = jnp.concatenate([high, low], axis=0)
    out = jnp.dot(both, weights, preferred_element_type=F32)
    upper = out[:size, :width]
    return upper + ((out[size:, :width] + out[:size, width:]) + out[size:, width:])


def body(
    n_row,
    n_col,
    values_hbm,
    index_ref,
    count_ref,
    strength_ref,
    raw_ref,
    packed_ref,
    *scratch,
):
    names = iter(scratch)
    take = lambda: next(names)
    each_step = lambda: [[take() for _ in range(PARTS)] for _ in range(ITERS)]
    stored, natural, turned, sums_row, sums_col = take(), take(), take(), take(), take()
    degree, direct, smooth = take(), take(), take()
    running = [take() for _ in range(PARTS)]
    got_rows, got_cols = each_step(), each_step()
    res_rows, res_cols = each_step(), each_step()
    row_send, col_send = each_step(), each_step()
    swap_got, row_sum = each_step(), each_step()
    row_got, col_got = each_step(), each_step()
    image = each_step()
    dot_own, dot_line = [take() for _ in range(ITERS)], [take() for _ in range(ITERS)]
    dot_col_got, dot_row_got = [take() for _ in range(ITERS)], [take() for _ in range(ITERS)]
    deg_row_send, deg_col_send, deg_row_got, deg_col_got = take(), take(), take(), take()
    gain_ref, listed, slots, scales, slots_at, scales_at = [take() for _ in range(6)]
    value_sem, plan_sem, sent, got = take(), take(), take(), take()

    a = lax.axis_index("row")
    c = lax.axis_index("col")
    core = lax.rem(c, 2)
    chip = c // 2
    sibling = c + 1 - 2 * core
    n_chip = n_col // 2
    far = sorted(range(1, n_chip), key=lambda k: -min(k, n_chip - k))
    cap = stored.shape[0]
    size = stored.shape[1]
    seg = raw_ref.shape[0]
    rhs = raw_ref.shape[1]
    share = rhs // PARTS
    n_local = n_col * seg
    n_other = n_row * seg
    GATHER_COL, GATHER_ROW, SWAP, PART_COL, PART_ROW = range(5)
    KINDS = 5
    DOTS = KINDS * PARTS * ITERS
    DEG_COL, DEG_ROW = DOTS + 2 * ITERS, DOTS + 2 * ITERS + 1
    sem_row = lambda step, part, kind: (step * PARTS + part) * KINDS + kind
    parts = range(PARTS)
    lanes = lambda part: slice(share * part, share * part + share)

    fetch = pltpu.make_async_copy(values_hbm.at[0, 0], stored, value_sem)
    fetch.start()

    barrier = pltpu.get_barrier_semaphore()

    def greet_col(k, _):
        pl.semaphore_signal(
            barrier, inc=1, device_id=(a, lax.rem(c + k, n_col)), device_id_type=MESH
        )
        return 0

    def greet_row(k, _):
        pl.semaphore_signal(
            barrier, inc=1, device_id=(lax.rem(a + k, n_row), c), device_id_type=MESH
        )
        return 0

    lax.fori_loop(1, n_col, greet_col, 0)
    lax.fori_loop(1, n_row, greet_row, 0)

    def send(src, dst, target, which, out_slot, in_slot):
        pltpu.make_async_remote_copy(
            src_ref=src,
            dst_ref=dst,
            send_sem=sent.at[which, out_slot],
            recv_sem=got.at[which, in_slot],
            device_id=target,
            device_id_type=MESH,
        ).start()

    def each_col(act):
        lax.fori_loop(1, n_col, lambda k, _: (act(lax.rem(c + k, n_col)), 0)[1], 0)

    def each_row(act):
        lax.fori_loop(1, n_row, lambda k, _: (act(lax.rem(a + k, n_row)), 0)[1], 0)

    def rows_below(act):
        lax.fori_loop(0, a, lambda k, _: (act(k), 0)[1], 0)

    def rows_above(act):
        lax.fori_loop(a + 1, n_row, lambda k, _: (act(k), 0)[1], 0)

    def other_chips(act):
        for k in far:
            act(lax.rem(chip + k, n_chip))

    def arrive(dst, which, slot):
        pltpu.make_async_copy(dst, dst, got.at[which, slot]).wait()

    def leave(src, which, slot):
        pltpu.make_async_copy(src, src, sent.at[which, slot]).wait()

    def gather(step, part):
        src = image[step][part]
        kind = sem_row(step, part, GATHER_COL)
        where = got_rows[step][part].at[pl.ds(seg * c, seg)]
        other_chips(lambda z: send(src, where, (a, 2 * z + core), kind, 0, c))
        send(src, where, (a, sibling), kind, 0, c)
        kind = sem_row(step, part, GATHER_ROW)
        where_col = got_cols[step][part].at[pl.ds(seg * a, seg)]
        rows_below(lambda r: send(src, where_col, (r, c), kind, r, a))
        got_rows[step][part][pl.ds(seg * c, seg)] = src[...]
        got_cols[step][part][pl.ds(seg * a, seg)] = src[...]

    def pass_on(step, part):
        kind = sem_row(step, part, GATHER_COL)
        for k in reversed(far):
            z = lax.rem(chip + k, n_chip)
            piece = got_rows[step][part].at[pl.ds(seg * (2 * z + core), seg)]
            arrive(piece, kind, 2 * z + core)
            send(piece, piece, (a, sibling), kind, 1, 2 * z + core)

    def from_sibling(step, part):
        kind = sem_row(step, part, GATHER_COL)
        for k in [0] + far[::-1]:
            z = lax.rem(chip + k, n_chip)
            slot = 2 * z + 1 - core
            arrive(got_rows[step][part].at[pl.ds(seg * slot, seg)], kind, slot)

    def sends_done(step):
        some = lambda ref, count: ref.at[pl.ds(0, count)]
        for part in parts:
            kind = sem_row(step, part, 0)
            leave(some(got_rows[step][part], seg * n_chip), kind + GATHER_COL, 0)
            leave(some(got_rows[step][part], seg * (n_chip - 1)), kind + GATHER_COL, 1)
            rows_below(lambda r: leave(image[step][part], kind + GATHER_ROW, r))
            leave(row_send[step][part].at[0], kind + SWAP, 0)
            leave(some(row_sum[step][part], seg * (n_chip - 1)), kind + PART_COL, 0)
            rows_above(lambda r: leave(some(col_send[step][part], seg), kind + PART_ROW, r))
        leave(some(dot_col_got[step], n_col - 1), DOTS + 2 * step, 0)
        leave(some(dot_row_got[step], n_row - 1), DOTS + 2 * step + 1, 0)

    for part in parts:
        image[0][part][...] = raw_ref[:, lanes(part), :]
    make_plan(index_ref, count_ref[...], cap, n_local, n_other, listed, slots, scales)
    to_slots = pltpu.make_async_copy(slots, slots_at, plan_sem.at[0])
    to_scales = pltpu.make_async_copy(scales, scales_at, plan_sem.at[1])
    to_slots.start()
    to_scales.start()
    for s in range(rhs):
        gain_ref[s : s + 1, :] = jnp.full((1, size), strength_ref[s], F32)
    fetch.wait()

    def prepare(q, _):
        block = stored[q]
        flipped = block.T
        high, low = split(block)
        natural[q, :, :size] = high
        natural[q, :, size:] = low
        high, low = split(flipped)
        turned[q, :, :size] = high
        turned[q, :, size:] = low
        sums_row[pl.ds(q, 1), :] = jnp.sum(flipped, axis=0, keepdims=True)
        sums_col[pl.ds(q, 1), :] = jnp.sum(block, axis=0, keepdims=True)
        return 0

    lax.fori_loop(0, cap // 2, prepare, 0, unroll=10)
    pl.semaphore_wait(barrier, n_col + n_row - 2)
    for part in parts:
        gather(0, part)
    lax.fori_loop(cap // 2, cap, prepare, 0, unroll=10)

    live = lax.broadcasted_iota(jnp.int32, (1, cap), 1) < count_ref[...]

    def pick(line, count):
        wanted = lax.broadcasted_iota(jnp.int32, (count, cap), 0)
        chosen = (wanted == index_ref[0, 0, line : line + 1, :]) & live
        return jnp.where(chosen, 1.0, 0.0)

    degree_rows = jnp.dot(
        pick(0, n_local), sums_row[...], precision=lax.Precision.HIGHEST, preferred_element_type=F32
    )
    degree_cols = jnp.dot(
        pick(1, n_other), sums_col[...], precision=lax.Precision.HIGHEST, preferred_element_type=F32
    )
    for peer in range(n_col):
        deg_row_send[peer] = degree_rows[seg * peer : seg * peer + seg, :]
    for peer in range(n_row):
        deg_col_send[peer] = degree_cols[seg * peer : seg * peer + seg, :]
    each_col(lambda p: send(deg_row_send.at[p], deg_row_got.at[c], (a, p), DEG_COL, 0, 0))
    rows_above(lambda r: send(deg_col_send.at[r], deg_col_got.at[a], (r, c), DEG_ROW, r, a))
    deg_row_got[c] = deg_row_send[c]
    deg_col_got[a] = deg_col_send[a]

    gains = gain_ref[...]
    to_slots.wait()
    to_scales.wait()

    def pass_over(weights, panel, side, out):
        def slot(k, total):
            weight = weights[slots_at[3 * side, k]]
            field = panel[slots_at[3 * side + 1, k]]
            total = total * scales_at[2 * side, k] + product(field, weight)
            out[k] = total
            return total

        lax.fori_loop(0, cap, slot, jnp.zeros((share, size), F32), unroll=True)

    def total_of(ref, count):
        out = ref[0]
        for k in range(1, count):
            out = out + ref[k]
        return out

    alphas, betas, gammas = [], [], []

    def finish_dots(step):
        arrive(dot_row_got[step].at[pl.ds(0, n_row - 1)], DOTS + 2 * step + 1, 0)
        dots = total_of(dot_row_got[step], n_row)
        dots = jnp.broadcast_to(dots, (size, size)).T
        gamma = dots[:rhs]
        delta = dots[rhs : 2 * rhs]
        if step == 0:
            alpha, beta = gamma / delta, None
        else:
            beta = gamma / gammas[-1]
            alpha = gamma / (delta - beta * gamma / alphas[-1])
        alphas.append(alpha)
        betas.append(beta)
        gammas.append(gamma)

    def form(step, part, fetched, formed, count):
        if step == 0:
            return fetched[0][part]
        alpha = alphas[step - 1][lanes(part)]
        before = fetched[0][part] if step == 1 else formed[step - 1][part]
        after = formed[step][part]

        if step == 1:
            def one(k, _):
                after[k] = before[k] - alpha * fetched[1][part][k]
                return 0
        else:
            beta = betas[step - 1][lanes(part)]

            def one(k, _):
                after[k] = before[k] - alpha * (fetched[2][part][k] + beta * fetched[1][part][k])
                return 0

        lax.fori_loop(0, count, one, 0, unroll=8)
        return after

    for step in range(ITERS):
        if step > 0:
            sends_done(step - 1)
            finish_dots(step - 1)
        gamma_part, delta_part, row_panels = [], [], []
        for part in parts:
            kind = sem_row(step, part, 0)
            pass_on(step, part)
            rows_above(lambda r: arrive(got_cols[step][part].at[pl.ds(seg * r, seg)], kind + GATHER_ROW, r))
            panel_cols = form(step, part, got_cols, res_cols, n_other)
            pass_over(turned, panel_cols, 0, running[part])
            for k in far + [0]:
                z = lax.rem(chip + k, n_chip)
                for half in range(2):
                    for j in range(seg):
                        u = seg * (2 * z + half) + j
                        row_send[step][part][half, seg * z + j] = (
                            running[part][slots_at[2, u]] * scales_at[1, u]
                        )
                piece = pl.ds(seg * z, seg)
                send(
                    row_send[step][part].at[1 - core, piece],
                    swap_got[step][part].at[piece],
                    (a, sibling),
                    kind + SWAP,
                    0,
                    z,
                )
            from_sibling(step, part)
            panel_rows = form(step, part, got_rows, res_rows, n_local)
            row_panels.append(panel_rows)
            if part == PARTS - 1 and step == ITERS - 1:
                if step == 0:
                    arrive(deg_row_got.at[pl.ds(0, n_col - 1)], DEG_COL, 0)
                    rows_below(lambda r: arrive(deg_col_got.at[r], DEG_ROW, r))
                    here = total_of(deg_row_got, n_col)
                    here = here + lax.fori_loop(
                        0, a + 1, lambda k, t: t + deg_col_got[k], jnp.zeros_like(here)
                    )
                    for j in range(seg):
                        degree[j] = jnp.broadcast_to(here[j : j + 1, :], (share, size))
                for p in parts:
                    cross = None
                    for u in range(n_local):
                        half, first = u // seg % 2, u // seg // 2 * seg
                        term = row_panels[p][u] * row_send[step][p][half, first + u % seg]
                        cross = term if cross is None else cross + term
                    square = [jnp.square(row_panels[p][seg * c + j]) for j in range(seg)]
                    gamma_part.append(functools.reduce(jnp.add, square))
                    rest = functools.reduce(jnp.add, [degree[j] * square[j] for j in range(seg)])
                    delta_part.append(gamma_part[p] + gains[lanes(p)] * (rest - 2.0 * cross))
                stack = jnp.concatenate(
                    gamma_part + delta_part + [jnp.zeros((size - 2 * rhs, size), F32)], axis=0
                )
                dot_own[step][...] = jnp.sum(stack.T, axis=0, keepdims=True)
                each_col(lambda p: send(dot_own[step], dot_col_got[step].at[c], (a, p), DOTS + 2 * step, 0, 0))
                dot_col_got[step][c] = dot_own[step][...]
            pass_over(natural, panel_rows, 1, running[part])
            for v in range(n_other):
                col_send[step][part][v] = running[part][slots_at[5, v]] * scales_at[3, v]
            rows_above(
                lambda r: send(
                    col_send[step][part].at[pl.ds(seg * r, seg)],
                    col_got[step][part].at[pl.ds(seg * a, seg)],
                    (r, c),
                    kind + PART_ROW,
                    r,
                    a,
                )
            )
            col_got[step][part][pl.ds(seg * a, seg)] = col_send[step][part][pl.ds(seg * a, seg)]
            if part == PARTS - 1 and step < ITERS - 1:
                if step == 0:
                    arrive(deg_row_got.at[pl.ds(0, n_col - 1)], DEG_COL, 0)
                    rows_below(lambda r: arrive(deg_col_got.at[r], DEG_ROW, r))
                    here = total_of(deg_row_got, n_col)
                    here = here + lax.fori_loop(
                        0, a + 1, lambda k, t: t + deg_col_got[k], jnp.zeros_like(here)
                    )
                    for j in range(seg):
                        degree[j] = jnp.broadcast_to(here[j : j + 1, :], (share, size))
                for p in parts:
                    cross = None
                    for u in range(n_local):
                        half, first = u // seg % 2, u // seg // 2 * seg
                        term = row_panels[p][u] * row_send[step][p][half, first + u % seg]
                        cross = term if cross is None else cross + term
                    square = [jnp.square(row_panels[p][seg * c + j]) for j in range(seg)]
                    gamma_part.append(functools.reduce(jnp.add, square))
                    rest = functools.reduce(jnp.add, [degree[j] * square[j] for j in range(seg)])
                    delta_part.append(gamma_part[p] + gains[lanes(p)] * (rest - 2.0 * cross))
                stack = jnp.concatenate(
                    gamma_part + delta_part + [jnp.zeros((size - 2 * rhs, size), F32)], axis=0
                )
                dot_own[step][...] = jnp.sum(stack.T, axis=0, keepdims=True)
                each_col(lambda p: send(dot_own[step], dot_col_got[step].at[c], (a, p), DOTS + 2 * step, 0, 0))
                dot_col_got[step][c] = dot_own[step][...]
            for k in far + [0]:
                z = lax.rem(chip + k, n_chip)
                piece = pl.ds(seg * z, seg)
                arrive(swap_got[step][part].at[piece], kind + SWAP, z)
                for j in range(seg):
                    row_sum[step][part][seg * z + j] = (
                        row_send[step][part][core, seg * z + j] + swap_got[step][part][seg * z + j]
                    )
                if k:
                    send(
                        row_sum[step][part].at[piece],
                        row_got[step][part].at[pl.ds(seg * chip, seg)],
                        (a, 2 * z + core),
                        kind + PART_COL,
                        0,
                        chip,
                    )

        fresh = []
        for part in parts:
            kind = sem_row(step, part, 0)
            if part == PARTS - 1:
                arrive(dot_col_got[step].at[pl.ds(0, n_col - 1)], DOTS + 2 * step, 0)
                dot_line[step][...] = total_of(dot_col_got[step], n_col)
                each_row(
                    lambda r: send(
                        dot_line[step], dot_row_got[step].at[a], (r, c), DOTS + 2 * step + 1, 0, 0
                    )
                )
                dot_row_got[step][a] = dot_line[step][...]
            rows_below(lambda r: arrive(col_got[step][part].at[pl.ds(seg * r, seg)], kind + PART_ROW, r))

            def add_cols(k, both):
                return tuple(both[j] + col_got[step][part][seg * k + j] for j in range(seg))

            spread = lax.fori_loop(
                0, a + 1, add_cols, tuple(row_sum[step][part][seg * chip + j] for j in range(seg))
            )
            spread = list(spread)
            for k in far[::-1]:
                z = lax.rem(chip + k, n_chip)
                arrive(row_got[step][part].at[pl.ds(seg * z, seg)], kind + PART_COL, z)
                for j in range(seg):
                    spread[j] = spread[j] + row_got[step][part][seg * z + j]
            w = []
            for j in range(seg):
                r = row_panels[part][seg * c + j]
                w.append(r + gains[lanes(part)] * (degree[j] * r - spread[j]))
            if step < ITERS - 1:
                for j in range(seg):
                    image[step + 1][part][j] = w[j]
                gather(step + 1, part)
            else:
                fresh.append(w)
        if step > 0:
            alpha, beta = alphas[step - 1], betas[step - 1]
            for part in parts:
                for j in range(seg):
                    own = (got_rows[0] if step == 1 else res_rows[step - 1])[part][seg * c + j]
                    if step == 1:
                        direct[j, lanes(part), :] = own
                        smooth[j, lanes(part), :] = alpha[lanes(part)] * own
                    else:
                        d = own + beta[lanes(part)] * direct[j, lanes(part), :]
                        direct[j, lanes(part), :] = d
                        smooth[j, lanes(part), :] = smooth[j, lanes(part), :] + alpha[lanes(part)] * d

    sends_done(ITERS - 1)
    leave(deg_row_got.at[pl.ds(0, n_col - 1)], DEG_COL, 0)
    rows_above(lambda r: leave(deg_col_send.at[r], DEG_ROW, r))
    finish_dots(ITERS - 1)
    for part in parts:
        alpha, beta = alphas[-1][lanes(part)], betas[-1][lanes(part)]
        for j in range(seg):
            r = row_panels[part][seg * c + j]
            slope = image[2][part][j] + betas[1][lanes(part)] * image[1][part][j]
            slope = fresh[part][j] + beta * slope
            d = r + beta * direct[j, lanes(part), :]
            packed_ref[0, j, lanes(part), :] = smooth[j, lanes(part), :] + alpha * d
            packed_ref[1, j, lanes(part), :] = r - alpha * slope


def make_plan(index_ref, count, cap, n_local, n_other, listed, slots, scales):
    width = listed.shape[1]
    listed[...] = jnp.zeros_like(listed)
    listed[0:2, 0:cap] = index_ref[0, 0]
    down = lax.broadcasted_iota(jnp.int32, (width, width), 0)
    across = lax.broadcasted_iota(jnp.int32, (width, width), 1)
    lines = [jnp.broadcast_to(listed[j : j + 1, :], (width, width)) for j in range(2)]
    turned = [line.T for line in lines]
    for side, groups in enumerate((n_local, n_other)):
        key = jnp.where(across < count, lines[side], groups) * width + across
        group = jnp.where(down < count, turned[side], groups)
        key_down = group * width + down
        rank = jnp.sum(jnp.where(key < key_down, 1, 0), axis=1, keepdims=True)
        at = rank == across
        total = lambda x: jnp.sum(x, axis=0, keepdims=True)
        ordered = total(jnp.where(at, group, 0))
        before = pltpu.roll(ordered, 1, 1)
        first = across[0:1, :] == 0
        below = total(jnp.where(group <= across, 1, 0))
        member = total(jnp.where(group == across, 1, 0))
        slots[3 * side : 3 * side + 1, :] = total(jnp.where(at, down, 0))
        slots[3 * side + 1 : 3 * side + 2, :] = total(jnp.where(at, turned[1 - side], 0))
        slots[3 * side + 2 : 3 * side + 3, :] = jnp.maximum(below - 1, 0)
        scales[2 * side : 2 * side + 1, :] = jnp.where((ordered == before) & ~first, 1.0, 0.0)
        scales[2 * side + 1 : 2 * side + 2, :] = jnp.where(member > 0, 1.0, 0.0)


def shards(n_row, n_col, block_values, block_index, block_count, strength, raw_scores):
    cap, size = block_values.shape[2], block_values.shape[3]
    seg, rhs, _ = raw_scores.shape
    n_local, n_other = n_col * seg, n_row * seg
    field = (seg, rhs, size)
    vmem = pl.BlockSpec(memory_space=pltpu.VMEM)
    smem = pl.BlockSpec(memory_space=pltpu.SMEM)
    n_chip = n_col // 2
    share = rhs // PARTS
    whole = lambda shape: [pltpu.VMEM(shape, F32)]
    many = lambda count: [pltpu.VMEM((count, share, size), F32) for _ in range(ITERS * PARTS)]
    scratch = [
        pltpu.VMEM((cap, size, size), F32),
        pltpu.VMEM((cap, size, 2 * size), BF16),
        pltpu.VMEM((cap, size, 2 * size), BF16),
        pltpu.VMEM((cap, size), F32),
        pltpu.VMEM((cap, size), F32),
        pltpu.VMEM((seg, share, size), F32),
        pltpu.VMEM(field, F32),
        pltpu.VMEM(field, F32),
    ]
    scratch += whole((cap, share, size)) * PARTS
    scratch += many(n_local) + many(n_other)
    scratch += many(n_local) + many(n_other)
    scratch += whole((2, n_chip * seg, share, size)) * (ITERS * PARTS) + many(n_other)
    scratch += many(n_chip * seg) + many(n_chip * seg)
    scratch += many(n_chip * seg) + many(n_other)
    scratch += many(seg)
    scratch += whole((1, size)) * (2 * ITERS)
    scratch += whole((n_col, 1, size)) * ITERS + whole((n_row, 1, size)) * ITERS
    scratch += [
        pltpu.VMEM((n_col, seg, size), F32),
        pltpu.VMEM((n_row, seg, size), F32),
        pltpu.VMEM((n_col, seg, size), F32),
        pltpu.VMEM((n_row, seg, size), F32),
    ]
    most = max(n_row, n_col)
    rows = 5 * PARTS * ITERS + 2 * ITERS + 2
    scratch += [
        pltpu.VMEM((rhs, size), F32),
        pltpu.VMEM((8, size), jnp.int32),
        pltpu.VMEM((8, size), jnp.int32),
        pltpu.VMEM((8, size), F32),
        pltpu.SMEM((8, size), jnp.int32),
        pltpu.SMEM((8, size), F32),
        pltpu.SemaphoreType.DMA,
        pltpu.SemaphoreType.DMA((2,)),
        pltpu.SemaphoreType.DMA((rows, most)),
        pltpu.SemaphoreType.DMA((rows, most)),
    ]
    packed = pl.pallas_call(
        functools.partial(body, n_row, n_col),
        out_shape=jax.ShapeDtypeStruct((2,) + field, F32),
        in_specs=[pl.BlockSpec(memory_space=pl.ANY), vmem, vmem, smem, vmem],
        out_specs=vmem,
        scratch_shapes=scratch,
        compiler_params=pltpu.CompilerParams(
            collective_id=0, has_side_effects=True, vmem_limit_bytes=56 * 1024 * 1024
        ),
    )(block_values, block_index, block_count, strength, raw_scores)
    return packed[0], packed[1]


def solution(mesh):
    n_row, n_col = mesh.shape["row"], mesh.shape["col"]
    placed = (
        P("row", "col", None, None, None),
        P("row", "col", None, None),
        P("row", "col"),
        P(),
        P(("row", "col"), None, None),
    )
    return jax.shard_map(
        functools.partial(shards, n_row, n_col),
        mesh=mesh,
        in_specs=placed,
        out_specs=(P(("row", "col"), None, None), P(("row", "col"), None, None)),
        check_vma=False,
    )
```
